128 devices in a mesh: row: 16 (over z, x_lo, core), col: 8 (over x_hi, y).
Axes of the slice: x: 4 (x_hi: 2, x_lo: 2; x = x_hi * 2 + x_lo), y: 4, z: 4, core: 2. Of those that a mesh axis runs over, the one named last changes fastest.
Arguments:
- tokens: bfloat16 [384, 8192], P(None, 'row'), may hold values from -6 to 6
- grad_out: bfloat16 [384, 8192], P(None, 'row'), may hold values from -6 to 6
- gate_weight: bfloat16 [8192, 22016], P('row', 'col'), may hold values from -0.0625 to 0.0625
- up_weight: bfloat16 [8192, 22016], P('row', 'col'), may hold values from -0.0625 to 0.0625
- down_weight: bfloat16 [8192, 22016], P('row', 'col'), may hold values from -0.0390625 to 0.0390625
- gate_left: bfloat16 [8192, 128], P('row', 'col'), may hold values from -0.01953125 to 0.01953125
- up_left: bfloat16 [8192, 128], P('row', 'col'), may hold values from -0.01953125 to 0.01953125
- down_left: bfloat16 [8192, 128], P('row', 'col'), may hold values from -0.01171875 to 0.01171875
- gate_right: bfloat16 [128, 22016], P('row', 'col'), may hold values from -0.5 to 0.5
- up_right: bfloat16 [128, 22016], P('row', 'col'), may hold values from -0.5 to 0.5
- down_right: bfloat16 [128, 22016], P('row', 'col'), may hold values from -0.5 to 0.5
Outputs:
- mixed: bfloat16 [384, 8192], P('col', 'row')
- input_grad: bfloat16 [384, 8192], P('col', 'row')
- gate_grad: bfloat16 [8192, 22016], P('row', 'col')
- up_grad: bfloat16 [8192, 22016], P('row', 'col')
- down_grad: bfloat16 [8192, 22016], P('row', 'col')
The draws below stay inside these ranges and needn't reach their ends.
All inputs are finite; a program needn't handle non-finite values.
Results may differ from the reference program's by a relative error of at most 0.0072.
Values may be sent and summed in bfloat16 or wider, within the bound.
No kernel may reach another device: no remote copies, remote signals or barrier semaphores. Data moves between devices by JAX's collectives and lax.ppermute only.
A program may use at most 128 MiB of HBM per device.

```python
import jax
import jax.numpy as jnp
from jax import lax

D = 8192
FF = 22016
R = 128
TOKENS = 384


def block_levels(key, shape, shards, least, high):
    def one(axis_at, shards_of):
        steps = jax.random.uniform(jax.random.fold_in(jax.random.fold_in(key, 6), axis_at), (shards_of,), jnp.float32, least / len(shards), high / len(shards))
        return jnp.repeat(jnp.exp(steps), shape[axis_at] // shards_of).reshape((-1,) + (1,) * (len(shape) - axis_at - 1))

    loudness = one(*shards[0])
    for cut in shards[1:]:
        loudness = loudness * one(*cut)
    return loudness


def bell_draw(own_key, dims, deviation, reach, split=(), dtype=jnp.bfloat16):
    entries = jax.random.normal(own_key, dims, jnp.float32) * deviation
    if len(split) > 0:
        entries = block_levels(own_key, dims, split, -0.22, 0.18) * entries
    return jnp.clip(entries, min=-reach, max=reach).astype(dtype)


def setup_inputs(seed: int = 0) -> dict:
    keys = jax.random.split(jax.random.key(seed), 12)
    tokens = bell_draw(keys[0], (TOKENS, D), 1.0, 6.0, ((1, 16),))
    grad_out = bell_draw(keys[1], (TOKENS, D), 1.0, 6.0, ((1, 16),))
    gate_weight = bell_draw(keys[2], (D, FF), D ** -0.5, 0.0625, ((0, 16), (1, 8)))
    up_weight = bell_draw(keys[3], (D, FF), D ** -0.5, 0.0625, ((0, 16), (1, 8)))
    down_weight = bell_draw(keys[4], (D, FF), FF ** -0.5, 0.0390625, ((0, 16), (1, 8)))
    gate_left = bell_draw(keys[5], (D, R), (D * 11) ** -0.5, 0.01953125, ((0, 16), (1, 8)))
    up_left = bell_draw(keys[6], (D, R), (D * 11) ** -0.5, 0.01953125, ((0, 16), (1, 8)))
    down_left = bell_draw(keys[7], (D, R), (FF * 11) ** -0.5, 0.01171875, ((0, 16), (1, 8)))
    gate_right = bell_draw(keys[8], (R, FF), R ** -0.5, 0.5, ((0, 16), (1, 8)))
    up_right = bell_draw(keys[9], (R, FF), R ** -0.5, 0.5, ((0, 16), (1, 8)))
    down_right = bell_draw(keys[10], (R, FF), R ** -0.5, 0.5, ((0, 16), (1, 8)))
    return {"tokens": tokens, "grad_out": grad_out, "gate_weight": gate_weight, "up_weight": up_weight, "down_weight": down_weight, "gate_left": gate_left, "up_left": up_left, "down_left": down_left, "gate_right": gate_right, "up_right": up_right, "down_right": down_right}


def merge_weight(base, left, right):
    delta = jnp.dot(left, right, preferred_element_type=jnp.float32)
    return (base.astype(jnp.float32) + delta).astype(jnp.bfloat16)


def reference(tokens, grad_out, gate_weight, up_weight, down_weight, gate_left, up_left, down_left, gate_right, up_right, down_right):
    merged_gate = merge_weight(gate_weight, gate_left, gate_right)
    merged_up = merge_weight(up_weight, up_left, up_right)
    merged_down = merge_weight(down_weight, down_left, down_right)
    gate = jnp.dot(tokens, merged_gate, preferred_element_type=jnp.float32)
    up = jnp.dot(tokens, merged_up, preferred_element_type=jnp.float32)
    sigma = jax.nn.sigmoid(gate)
    hidden = (gate * sigma * up).astype(jnp.bfloat16)
    last_dims = (((1,), (1,)), ((), ()))
    first_dims = (((0,), (0,)), ((), ()))
    mixed = lax.dot_general(hidden, merged_down, last_dims, preferred_element_type=jnp.float32).astype(jnp.bfloat16)
    back = jnp.dot(grad_out, merged_down, preferred_element_type=jnp.float32)
    gate_delta = (back * up * sigma * (1.0 + gate * (1.0 - sigma))).astype(jnp.bfloat16)
    up_delta = (back * gate * sigma).astype(jnp.bfloat16)
    input_grad = lax.dot_general(gate_delta, merged_gate, last_dims, preferred_element_type=jnp.float32)
    input_grad = input_grad + lax.dot_general(up_delta, merged_up, last_dims, preferred_element_type=jnp.float32)
    gate_grad = lax.dot_general(tokens, gate_delta, first_dims, preferred_element_type=jnp.float32).astype(jnp.bfloat16)
    up_grad = lax.dot_general(tokens, up_delta, first_dims, preferred_element_type=jnp.float32).astype(jnp.bfloat16)
    down_grad = lax.dot_general(grad_out, hidden, first_dims, preferred_element_type=jnp.float32).astype(jnp.bfloat16)
    return mixed, input_grad.astype(jnp.bfloat16), gate_grad, up_grad, down_grad
```

```python
import jax
import jax.numpy as jnp
from jax import lax
from jax.sharding import PartitionSpec as P

BF = jnp.bfloat16
F32 = jnp.float32
ROWS = 24


def dot(a, b, dims):
    return lax.dot_general(a, b, (dims, ((), ())), preferred_element_type=F32)


NN = ((1,), (0,))
NT = ((1,), (1,))
TN = ((0,), (0,))


def row_send(x, dz, da, dc):
    pairs = []
    for z in range(4):
        for a in range(2):
            for c in range(2):
                to = ((z + dz) % 4) * 4 + ((a + da) % 2) * 2 + (c + dc) % 2
                pairs.append((z * 4 + a * 2 + c, to))
    return lax.ppermute(x, "row", pairs)


def col_send(x, dh, dy):
    pairs = []
    for h in range(2):
        for y in range(4):
            pairs.append((h * 4 + y, ((h + dh) % 2) * 4 + (y + dy) % 4))
    return lax.ppermute(x, "col", pairs)


def row_reduce(mine, theirs, z_first):
    n = mine.shape[1]
    got = row_send(theirs, 0, 0, 1)
    total = (mine + got.astype(F32)).reshape(4, 2, ROWS, n)
    if z_first:
        own = total[0]
        parts = [row_send(total[d].astype(BF), d, 0, 0) for d in (1, 3, 2)]
        for p in parts:
            own = own + p.astype(F32)
        return own[0] + row_send(own[1].astype(BF), 0, 1, 0).astype(F32)
    own = total[:, 0] + row_send(total[:, 1].astype(BF), 0, 1, 0).astype(F32)
    parts = [row_send(own[d].astype(BF), d, 0, 0) for d in (1, 3, 2)]
    own = own[0]
    for p in parts:
        own = own + p.astype(F32)
    return own


def row_gather(x, z_last):
    rows, n = x.shape
    if z_last:
        pair = jnp.stack([x, row_send(x, 0, 1, 0)])
        got = {d: row_send(pair, d, 0, 0) for d in (1, 3, 2)}
        half = jnp.stack([pair, got[3], got[2], got[1]])
    else:
        got = {d: row_send(x, d, 0, 0) for d in (1, 3, 2)}
        four = jnp.stack([x, got[3], got[2], got[1]])
        half = jnp.stack([four, row_send(four, 0, 1, 0)], axis=1)
    half = half.reshape(8 * rows, n)
    return jnp.concatenate([half, row_send(half, 0, 0, 1)], axis=0)


def col_reduce(part, order):
    spread = dot(order, part.astype(BF), NN).astype(BF).reshape(2, 4, 48, -1)
    own = spread[0].astype(F32) + col_send(spread[1], 1, 0).astype(F32)
    parts = [col_send(own[d].astype(BF), 0, d) for d in (1, 3, 2)]
    own = own[0]
    for p in parts:
        own = own + p.astype(F32)
    return own.astype(BF)


def shards(
    tokens,
    grad_out,
    gate_weight,
    up_weight,
    down_weight,
    gate_left,
    up_left,
    down_left,
    gate_right,
    up_right,
    down_right,
):
    n = gate_weight.shape[1]
    row, col = lax.axis_index("row"), lax.axis_index("col")
    z, a, c = row // 4, (row // 2) % 2, row % 2
    h, y = col // 4, col % 4

    def local_block(k):
        dc, dz, da = k // 8, (k // 2) % 4, k % 2
        return (z + dz) % 4, (a + da) % 2, (c + dc) % 2

    k = jnp.arange(384)
    bz, ba, bc = local_block(k // ROWS)
    held = ((bc * 4 + bz) * 2 + ba) * ROWS + k % ROWS
    order = (held[:, None] == k[None, :]).astype(BF)
    dest = ((h + k // 192) % 2) * 4 + (y + (k // 48) % 4) % 4
    leave = ((dest * 48 + k % 48)[:, None] == held[None, :]).astype(BF)

    j = jnp.arange(128)
    rz, ra, rc = local_block(j // 8)
    right_rank = (rz * 4 + ra * 2 + rc) * 8 + j % 8
    m = jnp.arange(384)
    my, mh, mt, mi = (m // 96), (m // 48) % 2, (m // 16) % 3, m % 16
    left_rank = (((h - mh) % 2) * 4 + (y - my) % 4) * 16 + mi
    match = ((left_rank + 128 * mt)[None, :] == m[:, None]).astype(BF)
    sort = (right_rank[None, :] == j[:, None]).astype(BF)

    rights = row_gather(jnp.concatenate([gate_right, up_right, down_right], axis=1), True)
    rights = dot(sort, rights, NN).astype(BF)
    right_g, right_u, right_d = (rights[:, n * t : n * (t + 1)] for t in range(3))
    lefts = jnp.concatenate([gate_left.T, up_left.T, down_left.T], axis=0)
    lefts = jnp.stack([lefts, col_send(lefts, 1, 0)])
    lefts = jnp.stack([lefts] + [col_send(lefts, 0, d) for d in (1, 2, 3)])
    lefts = dot(match, lefts.reshape(384, 512), NN).astype(BF)

    tok = dot(order, tokens, NN).astype(BF)
    out = dot(order, grad_out, NN).astype(BF)

    def halves(x, w):
        return dot(x[:192], w, NN), dot(x[192:], w, NN).astype(BF)

    gate_rows = row_reduce(*halves(tok, gate_weight), False)
    low = jnp.concatenate([dot(tok, lefts[:256], NT), dot(out, lefts[256:], NT)], axis=1)
    up_mine, up_theirs = halves(tok, up_weight)
    up_rows = row_reduce(
        jnp.concatenate([low[:192], up_mine], axis=1),
        jnp.concatenate([low[192:].astype(BF), up_theirs], axis=1),
        True,
    )
    back_rows = row_reduce(*halves(out, down_weight), False)
    low = up_rows[:, :384].astype(BF)
    gate = gate_rows + dot(low[:, :128], right_g, NN)
    up = up_rows[:, 384:] + dot(low[:, 128:256], right_u, NN)
    back = back_rows + dot(low[:, 256:], right_d, NN)

    sigma = jax.nn.sigmoid(gate)
    hidden = row_gather((gate * sigma * up).astype(BF), True)
    gate_delta = (back * up * sigma * (1.0 + gate * (1.0 - sigma))).astype(BF)
    up_delta = (back * gate * sigma).astype(BF)
    gate_delta = row_gather(gate_delta, False)
    up_delta = row_gather(up_delta, True)

    def through(x, w, right, left):
        return dot(x, w, NT) + dot(dot(x, right, NT).astype(BF), left, NN)

    mixed = col_reduce(through(hidden, down_weight, right_d, lefts[256:]), leave)
    input_grad = col_reduce(
        through(gate_delta, gate_weight, right_g, lefts[:128])
        + through(up_delta, up_weight, right_u, lefts[128:256]),
        leave,
    )
    gate_grad = dot(tok, gate_delta, TN).astype(BF)
    up_grad = dot(tok, up_delta, TN).astype(BF)
    down_grad = dot(out, hidden, TN).astype(BF)
    return mixed, input_grad, gate_grad, up_grad, down_grad


def solution(mesh):
    arg = P("row", "col")
    in_specs = (P(None, "row"), P(None, "row")) + (arg,) * 9
    out_specs = (P("col", "row"), P("col", "row")) + (arg,) * 3
    return jax.shard_map(shards, mesh=mesh, in_specs=in_specs, out_specs=out_specs, check_vma=False)
```

```python
import jax
import jax.numpy as jnp
from jax import lax
from jax.experimental import pallas as pl
from jax.experimental.pallas import tpu as pltpu
from jax.sharding import PartitionSpec as P

BF = jnp.bfloat16
F32 = jnp.float32
ROWS = 24
HALF = 192
CHUNK = 512
RANK = 128
LIMIT = 48 * 1024 * 1024

NN = ((1,), (0,))
NT = ((1,), (1,))
TN = ((0,), (0,))


def dot(a, b, dims):
    return lax.dot_general(a, b, (dims, ((), ())), preferred_element_type=F32)


def after(x, *others):
    return lax.optimization_barrier((x,) + others)[0]


def chunks(n):
    return [(at, min(CHUNK, n - at)) for at in range(0, n, CHUNK)]


def pick(index_ref, size):
    return (index_ref[...] == lax.broadcasted_iota(jnp.int32, (size, size), 1)).astype(BF)


VMEM = pl.BlockSpec(memory_space=pltpu.VMEM)
ANY = pl.BlockSpec(memory_space=pl.ANY)


def forward(x, weight, index=None, lefts=None):
    n = weight.shape[0]
    low = 0 if lefts is None else lefts.shape[0]
    size, depth = x.shape

    def body(*refs):
        refs = list(refs)
        x_ref = refs.pop(0)
        index_ref = None if index is None else refs.pop(0)
        left_ref = None if lefts is None else refs.pop(0)
        w_hbm = refs.pop(0)
        mine_ref, theirs_ref = refs.pop(0), refs.pop(0)
        turned_ref = None if index is None else refs.pop(0)
        w_ref, sems = refs
        copies = []
        for k, (at, wide) in enumerate(chunks(n)):
            part = pl.ds(at, wide)
            copies.append(pltpu.make_async_copy(w_hbm.at[part, :], w_ref.at[part, :], sems.at[k]))
            copies[-1].start()
        if index is None:
            value = x_ref[...]
        else:
            value = dot(pick(index_ref, size), x_ref[...], NN).astype(BF)
            turned_ref[...] = value
        if lefts is not None:
            got = dot(value, left_ref[...], NT)
            mine_ref[:, :low] = got[:HALF]
            theirs_ref[:, :low] = got[HALF:].astype(BF)
        for copy, (at, wide) in zip(copies, chunks(n)):
            copy.wait()
            got = dot(value, w_ref[at : at + wide, :], NT)
            mine_ref[:, low + at : low + at + wide] = got[:HALF]
            theirs_ref[:, low + at : low + at + wide] = got[HALF:].astype(BF)

    args, specs = [x], [VMEM]
    if index is not None:
        args.append(index)
        specs.append(VMEM)
    if lefts is not None:
        args.append(lefts)
        specs.append(VMEM)
    out = [jax.ShapeDtypeStruct((HALF, low + n), F32), jax.ShapeDtypeStruct((HALF, low + n), BF)]
    if index is not None:
        out.append(jax.ShapeDtypeStruct((size, depth), BF))
    return pl.pallas_call(
        body,
        out_shape=out,
        in_specs=specs + [ANY],
        out_specs=[VMEM] * len(out),
        scratch_shapes=[pltpu.VMEM((n, depth), BF), pltpu.SemaphoreType.DMA((len(chunks(n)),))],
        compiler_params=pltpu.CompilerParams(vmem_limit_bytes=LIMIT),
        name="forward",
    )(*args, weight)


def backward(mine, other, x, weight, rights, lefts, place, partial=None, index=None):
    n, depth = weight.shape
    size = 2 * HALF
    padded = rights.shape[1] // 3

    def body(*refs):
        refs = list(refs)
        mine_ref, other_ref, x_ref, right_ref, left_ref = refs[:5]
        refs = refs[5:]
        partial_ref = None if partial is None else refs.pop(0)
        index_ref = None if index is None else refs.pop(0)
        w_hbm, out_ref, grad_hbm, w_ref, grad_ref, w_sems, sems = refs
        copies = []
        for k, (at, wide) in enumerate(chunks(n)):
            part = pl.ds(at, wide)
            copies.append(pltpu.make_async_copy(w_hbm.at[part, :], w_ref.at[part, :], w_sems.at[k]))
            copies[-1].start()
        total = jnp.zeros((size, depth), F32) if partial is None else partial_ref[...]
        low = jnp.zeros((size, RANK), F32)
        x_all = x_ref[...]
        sent = []
        for k, (at, wide) in enumerate(chunks(n)):
            part = pl.ds(at, wide)
            value = jnp.concatenate([mine_ref[:, at : at + wide], other_ref[:, at : at + wide]], axis=0)
            grad_ref[at : at + wide, :] = dot(value, x_all, TN).astype(BF)
            sent.append(pltpu.make_async_copy(grad_ref.at[part, :], grad_hbm.at[part, :], sems.at[k]))
            sent[-1].start()
            low = low + dot(value, right_ref[:, at : at + wide], NT)
            copies[k].wait()
            total = total + dot(value, w_ref[at : at + wide, :], NN)
        total = total + dot(low.astype(BF), left_ref[...], NN)
        if index is None:
            out_ref[...] = total
        else:
            out_ref[...] = dot(pick(index_ref, size), total.astype(BF), NN).astype(BF)
        for copy in sent:
            copy.wait()

    args, specs = [mine, other, x, rights, lefts], [
        VMEM,
        VMEM,
        VMEM,
        pl.BlockSpec((RANK, padded), lambda i: (0, place)),
        pl.BlockSpec((RANK, depth), lambda i: (place, 0)),
    ]
    if partial is not None:
        args.append(partial)
        specs.append(VMEM)
    if index is not None:
        args.append(index)
        specs.append(VMEM)
    count = len(chunks(n))
    return pl.pallas_call(
        body,
        grid=(1,),
        out_shape=[
            jax.ShapeDtypeStruct((size, depth), F32 if index is None else BF),
            jax.ShapeDtypeStruct((n, depth), BF),
        ],
        in_specs=specs + [ANY],
        out_specs=[VMEM, ANY],
        scratch_shapes=[
            pltpu.VMEM((n, depth), BF),
            pltpu.VMEM((n, depth), BF),
            pltpu.SemaphoreType.DMA((count,)),
            pltpu.SemaphoreType.DMA((count,)),
        ],
        compiler_params=pltpu.CompilerParams(vmem_limit_bytes=LIMIT),
        name="backward",
    )(*args, weight)


def row_send(x, dz, da, dc):
    pairs = []
    for z in range(4):
        for a in range(2):
            for c in range(2):
                to = ((z + dz) % 4) * 4 + ((a + da) % 2) * 2 + (c + dc) % 2
                pairs.append((z * 4 + a * 2 + c, to))
    return lax.ppermute(x, "row", pairs)


def col_send(x, dh, dy):
    pairs = []
    for h in range(2):
        for y in range(4):
            pairs.append((h * 4 + y, ((h + dh) % 2) * 4 + (y + dy) % 4))
    return lax.ppermute(x, "col", pairs)


def pair_sum(mine, theirs):
    return (mine + row_send(theirs, 0, 0, 1).astype(F32)).reshape(4, 2, ROWS, -1)


def row_reduce(total, z_first):
    if z_first:
        own = total[0]
        parts = [row_send(total[d].astype(BF), d, 0, 0) for d in (1, 3, 2)]
        for p in parts:
            own = own + p.astype(F32)
        return own[0] + row_send(own[1].astype(BF), 0, 1, 0).astype(F32)
    own = total[:, 0] + row_send(total[:, 1].astype(BF), 0, 1, 0).astype(F32)
    parts = [row_send(own[d].astype(BF), d, 0, 0) for d in (1, 3, 2)]
    own = own[0]
    for p in parts:
        own = own + p.astype(F32)
    return own


def row_gather(x, z_last):
    rows, n = x.shape
    if z_last:
        pair = jnp.stack([x, row_send(x, 0, 1, 0)])
        got = {d: row_send(pair, d, 0, 0) for d in (1, 3, 2)}
        half = jnp.stack([pair, got[3], got[2], got[1]])
    else:
        got = {d: row_send(x, d, 0, 0) for d in (1, 3, 2)}
        four = jnp.stack([x, got[3], got[2], got[1]])
        half = jnp.stack([four, row_send(four, 0, 1, 0)], axis=1)
    half = half.reshape(8 * rows, n)
    return half, row_send(half, 0, 0, 1)


def col_reduce(spread):
    spread = spread.reshape(2, 4, 48, -1)
    own = spread[0].astype(F32) + col_send(spread[1], 1, 0).astype(F32)
    parts = [col_send(own[d].astype(BF), 0, d) for d in (1, 3, 2)]
    own = own[0]
    for p in parts:
        own = own + p.astype(F32)
    return own.astype(BF)


def shards(
    tokens,
    grad_out,
    gate_weight,
    up_weight,
    down_weight,
    gate_left,
    up_left,
    down_left,
    gate_right,
    up_right,
    down_right,
):
    n = gate_weight.shape[1]
    row, col = lax.axis_index("row"), lax.axis_index("col")
    z, a, c = row // 4, (row // 2) % 2, row % 2
    h, y = col // 4, col % 4

    k = jnp.arange(2 * HALF, dtype=jnp.int32)
    block = k // ROWS
    dc, dz, da = block // 8, (block // 2) % 4, block % 2
    held = ((((c + dc) % 2) * 4 + (z + dz) % 4) * 2 + (a + da) % 2) * ROWS + k % ROWS
    dest = (((h + k // 192) % 2) * 4 + (y + k // 48) % 4) * 48 + k % 48
    block = dest // ROWS
    dc, dz, da = (block // 8 - c) % 2, ((block // 2) % 4 - z) % 4, (block % 2 - a) % 2
    leave = ((dc * 4 + dz) * 2 + da) * ROWS + dest % ROWS
    held, leave = held[:, None], leave[:, None]
    my, mh, mt, mi = k // 96, (k // 48) % 2, (k // 16) % 3, k % 16
    rank = (((h - mh) % 2) * 4 + (y - my) % 4) * 16 + mi + RANK * mt
    match = (rank[None, :] == k[:, None]).astype(BF)

    edge = jnp.zeros((gate_right.shape[0], -n % 128), BF)
    rights = jnp.concatenate([gate_right, edge, up_right, edge, down_right, edge], axis=1)
    rights = lax.all_gather(rights, "row", axis=0, tiled=True)
    wide = rights.shape[1] // 3

    gate_w, up_w, down_w = gate_weight.T, up_weight.T, down_weight.T
    gate_mine, gate_theirs, tok = forward(tokens, gate_w, index=held)

    lefts = jnp.concatenate([gate_left.T, up_left.T, down_left.T], axis=0)
    lefts = jnp.stack([lefts, col_send(lefts, 1, 0)])
    gate_sum = pair_sum(gate_mine, gate_theirs)
    lefts = after(lefts, gate_sum)
    lefts = jnp.stack([lefts] + [col_send(lefts, 0, d) for d in (1, 2, 3)])
    lefts = dot(match, lefts.reshape(3 * RANK, -1), NN).astype(BF)

    gate_rows = row_reduce(gate_sum, False)
    up_mine, up_theirs = forward(tok, up_w, lefts=lefts[: 2 * RANK])
    back_mine, back_theirs, out = forward(
        after(grad_out, up_theirs), down_w, index=held, lefts=lefts[2 * RANK :]
    )
    up_rows = row_reduce(pair_sum(up_mine, up_theirs), True)
    back_rows = row_reduce(pair_sum(back_mine, back_theirs), False)

    low_g, low_u = up_rows[:, :RANK].astype(BF), up_rows[:, RANK : 2 * RANK].astype(BF)
    low_d = back_rows[:, :RANK].astype(BF)
    gate = gate_rows + dot(low_g, rights[:, :n], NN)
    up = up_rows[:, 2 * RANK :] + dot(low_u, rights[:, wide : wide + n], NN)
    hidden = (gate * jax.nn.sigmoid(gate) * up).astype(BF)
    gate, up, back_rows, _ = lax.optimization_barrier((gate, up, back_rows, hidden))
    hidden = row_gather(hidden, True)

    back = back_rows[:, RANK:] + dot(low_d, rights[:, 2 * wide : 2 * wide + n], NN)
    sigma = jax.nn.sigmoid(gate)
    gate_delta = (back * up * sigma * (1.0 + gate * (1.0 - sigma))).astype(BF)
    up_delta = (back * gate * sigma).astype(BF)
    gate_delta = row_gather(gate_delta, False)
    up_delta = row_gather(up_delta, True)

    mixed, down_grad = backward(*hidden, out, down_w, rights, lefts, 2, index=leave)
    mixed = col_reduce(mixed)
    partial, gate_grad = backward(*gate_delta, tok, gate_w, rights, lefts, 0)
    input_grad, up_grad = backward(*up_delta, tok, up_w, rights, lefts, 1, partial=partial, index=leave)
    input_grad = col_reduce(input_grad)
    return mixed, input_grad, gate_grad.T, up_grad.T, down_grad.T


def solution(mesh):
    arg = P("row", "col")
    in_specs = (P(None, "row"), P(None, "row")) + (arg,) * 9
    out_specs = (P("col", "row"), P("col", "row")) + (arg,) * 3
    return jax.shard_map(shards, mesh=mesh, in_specs=in_specs, out_specs=out_specs, check_vma=False)
```

```python
import jax
import jax.numpy as jnp
from jax import lax
from jax.experimental import pallas as pl
from jax.experimental.pallas import tpu as pltpu
from jax.sharding import PartitionSpec as P

BF = jnp.bfloat16
F32 = jnp.float32
ROWS = 24
HALF = 192
CHUNK = 256
RANK = 128
LOW = 512
LIMIT = 48 * 1024 * 1024

NN = ((1,), (0,))
NT = ((1,), (1,))
TN = ((0,), (0,))


def dot(a, b, dims):
    return lax.dot_general(a, b, (dims, ((), ())), preferred_element_type=F32)


def after(x, *others):
    return lax.optimization_barrier((x,) + others)[0]


def pick(index_ref, size):
    return (index_ref[...] == lax.broadcasted_iota(jnp.int32, (size, size), 1)).astype(BF)


VMEM = pl.BlockSpec(memory_space=pltpu.VMEM)
ANY = pl.BlockSpec(memory_space=pl.ANY)
COST = pl.CostEstimate(flops=1024, bytes_accessed=1024, transcendentals=0)


def copy_in(src, dst, sems, k, at, wide):
    part = pl.ds(at, wide)
    return pltpu.make_async_copy(src.at[part, :], dst.at[part, :], sems.at[k])


def sweep(n, step):
    whole = n // CHUNK

    def body(k, _):
        step(k, pl.multiple_of(k * CHUNK, 128), CHUNK)
        return 0

    lax.fori_loop(0, whole, body, 0)
    if n % CHUNK:
        step(whole, whole * CHUNK, n % CHUNK)


def chunks(n):
    return -(-n // CHUNK)


def params():
    return pltpu.CompilerParams(vmem_limit_bytes=LIMIT)


def forward_first(tokens, grad_out, index, lefts, weight):
    n, depth = weight.shape
    size = tokens.shape[0]
    rank = lefts[0].shape[0]

    def body(t_ref, g_ref, i_ref, lg_ref, lu_ref, ld_ref, w_hbm, mine_ref, theirs_ref, tok_ref, out_ref, low_ref, w_ref, sems):
        for k in range(chunks(n)):
            copy_in(w_hbm, w_ref, sems, k, k * CHUNK, min(CHUNK, n - k * CHUNK)).start()
        turn = pick(i_ref, size)
        tok_ref[...] = dot(turn, t_ref[...], NN).astype(BF)

        def step(k, at, wide):
            copy_in(w_hbm, w_ref, sems, k, at, wide).wait()
            got = dot(tok_ref[...], w_ref[pl.ds(at, wide), :], NT)
            mine_ref[:, pl.ds(at, wide)] = got[:HALF]
            theirs_ref[:, pl.ds(at, wide)] = got[HALF:].astype(BF)

        sweep(n, step)
        out_ref[...] = dot(turn, g_ref[...], NN).astype(BF)
        none = jnp.zeros((RANK - 2 * rank, depth), BF)
        low = dot(t_ref[...], jnp.concatenate([lg_ref[...], lu_ref[...], none], axis=0), NT)
        none = jnp.zeros((rank, depth), BF)
        down = [none, none, ld_ref[...]] + [none] * (RANK // rank - 3)
        low = low + dot(g_ref[...], jnp.concatenate(down, axis=0), NT)
        low_ref[...] = low.astype(BF)

    return pl.pallas_call(
        body,
        out_shape=[
            jax.ShapeDtypeStruct((HALF, n), F32),
            jax.ShapeDtypeStruct((HALF, n), BF),
            jax.ShapeDtypeStruct((size, depth), BF),
            jax.ShapeDtypeStruct((size, depth), BF),
            jax.ShapeDtypeStruct((size, RANK), BF),
        ],
        in_specs=[VMEM] * 6 + [ANY],
        out_specs=[VMEM] * 5,
        scratch_shapes=[pltpu.VMEM((n, depth), BF), pltpu.SemaphoreType.DMA((chunks(n),))],
        compiler_params=params(),
        cost_estimate=COST,
        name="forward_first",
    )(tokens, grad_out, index, *lefts, weight)


def forward(x, weight):
    n, depth = weight.shape

    def body(x_ref, w_hbm, mine_ref, theirs_ref, w_ref, sems):
        for k in range(chunks(n)):
            copy_in(w_hbm, w_ref, sems, k, k * CHUNK, min(CHUNK, n - k * CHUNK)).start()

        def step(k, at, wide):
            copy_in(w_hbm, w_ref, sems, k, at, wide).wait()
            got = dot(x_ref[...], w_ref[pl.ds(at, wide), :], NT)
            mine_ref[:, pl.ds(at, wide)] = got[:HALF]
            theirs_ref[:, pl.ds(at, wide)] = got[HALF:].astype(BF)

        sweep(n, step)

    return pl.pallas_call(
        body,
        out_shape=[jax.ShapeDtypeStruct((HALF, n), F32), jax.ShapeDtypeStruct((HALF, n), BF)],
        in_specs=[VMEM, ANY],
        out_specs=[VMEM] * 2,
        scratch_shapes=[pltpu.VMEM((n, depth), BF), pltpu.SemaphoreType.DMA((chunks(n),))],
        compiler_params=params(),
        cost_estimate=COST,
        name="forward",
    )(x, weight)


def halves(mine_ref, other_ref, at, wide):
    part = pl.ds(at, wide)
    return jnp.concatenate([mine_ref[:, part], other_ref[:, part]], axis=0)


def product(mine, other, weight, rights, lefts, place, partial=None, index=None):
    n, depth = weight.shape
    size = 2 * HALF
    padded = rights.shape[1] // 3

    def body(*refs):
        refs = list(refs)
        mine_ref, other_ref, right_ref, left_ref = refs[:4]
        refs = refs[4:]
        partial_ref = None if partial is None else refs.pop(0)
        index_ref = None if index is None else refs.pop(0)
        w_hbm, out_ref, w_ref, total_ref, low_ref, sems = refs
        for k in range(chunks(n)):
            copy_in(w_hbm, w_ref, sems, k, k * CHUNK, min(CHUNK, n - k * CHUNK)).start()
        total_ref[...] = jnp.zeros((size, depth), F32) if partial is None else partial_ref[...]
        low_ref[...] = jnp.zeros((size, RANK), F32)

        def step(k, at, wide):
            value = halves(mine_ref, other_ref, at, wide)
            low_ref[...] += dot(value, right_ref[:, pl.ds(at, wide)], NT)
            copy_in(w_hbm, w_ref, sems, k, at, wide).wait()
            total_ref[...] += dot(value, w_ref[pl.ds(at, wide), :], NN)

        sweep(n, step)
        total = total_ref[...] + dot(low_ref[...].astype(BF), left_ref[...], NN)
        if index is None:
            out_ref[...] = total
        else:
            out_ref[...] = dot(pick(index_ref, size), total.astype(BF), NN).astype(BF)

    args = [mine, other, rights, lefts]
    specs = [
        VMEM,
        VMEM,
        pl.BlockSpec((RANK, padded), lambda i: (0, place)),
        pl.BlockSpec((RANK, depth), lambda i: (place, 0)),
    ]
    if partial is not None:
        args.append(partial)
        specs.append(VMEM)
    if index is not None:
        args.append(index)
        specs.append(VMEM)
    return pl.pallas_call(
        body,
        grid=(1,),
        out_shape=jax.ShapeDtypeStruct((size, depth), F32 if index is None else BF),
        in_specs=specs + [ANY],
        out_specs=VMEM,
        scratch_shapes=[
            pltpu.VMEM((n, depth), BF),
            pltpu.VMEM((size, depth), F32),
            pltpu.VMEM((size, RANK), F32),
            pltpu.SemaphoreType.DMA((chunks(n),)),
        ],
        compiler_params=params(),
        cost_estimate=COST,
        name="product",
    )(*args, weight)


def weight_grad(mine, other, x):
    n, depth = mine.shape[1], x.shape[1]

    def body(mine_ref, other_ref, x_ref, grad_hbm, grad_ref, sems):
        def step(k, at, wide):
            value = halves(mine_ref, other_ref, at, wide)
            grad_ref[pl.ds(at, wide), :] = dot(value, x_ref[...], TN).astype(BF)
            copy_in(grad_ref, grad_hbm, sems, k, at, wide).start()

        sweep(n, step)
        for k in range(chunks(n)):
            copy_in(grad_ref, grad_hbm, sems, k, k * CHUNK, min(CHUNK, n - k * CHUNK)).wait()

    return pl.pallas_call(
        body,
        out_shape=jax.ShapeDtypeStruct((n, depth), BF),
        in_specs=[VMEM] * 3,
        out_specs=ANY,
        scratch_shapes=[pltpu.VMEM((n, depth), BF), pltpu.SemaphoreType.DMA((chunks(n),))],
        compiler_params=params(),
        cost_estimate=COST,
        name="weight_grad",
    )(mine, other, x)


def act(gate, up, up_x, low, rights):
    rows, n = up.shape
    wide = rights.shape[1] // 3

    def body(g_ref, u_ref, x_ref, low_ref, right_ref, gate_ref, up_ref, hidden_ref):
        def step(k, at, size):
            part = pl.ds(at, size)
            lg = dot(low_ref[:RANK, LOW:], right_ref[:, part], TN)[:rows]
            lu = dot(low_ref[RANK : 2 * RANK, LOW:], right_ref[:, pl.ds(wide + at, size)], TN)[:rows]
            g = g_ref[:, part] + lg
            u = u_ref[:, part] + x_ref[:, part].astype(F32) + lu
            gate_ref[:, part] = g
            up_ref[:, part] = u
            hidden_ref[:, part] = (g * jax.nn.sigmoid(g) * u).astype(BF)

        sweep(n, step)

    return pl.pallas_call(
        body,
        out_shape=[jax.ShapeDtypeStruct((rows, n), t) for t in (F32, F32, BF)],
        in_specs=[VMEM] * 5,
        out_specs=[VMEM] * 3,
        compiler_params=params(),
        cost_estimate=COST,
        name="act",
    )(gate, up, up_x, low, rights)


def derive(gate, up, back, parts, low, rights):
    rows, n = up.shape
    wide = rights.shape[1] // 3

    def body(g_ref, u_ref, b_ref, p_ref, q_ref, r_ref, low_ref, right_ref, gd_ref, ud_ref):
        def step(k, at, size):
            part = pl.ds(at, size)
            b = dot(low_ref[2 * RANK :, LOW:], right_ref[:, pl.ds(2 * wide + at, size)], TN)[:rows]
            b = b + b_ref[:, part]
            for ref in (p_ref, q_ref, r_ref):
                b = b + ref[:, part].astype(F32)
            g, u = g_ref[:, part], u_ref[:, part]
            sigma = jax.nn.sigmoid(g)
            gd_ref[:, part] = (b * u * sigma * (1.0 + g * (1.0 - sigma))).astype(BF)
            ud_ref[:, part] = (b * g * sigma).astype(BF)

        sweep(n, step)

    return pl.pallas_call(
        body,
        out_shape=[jax.ShapeDtypeStruct((rows, n), BF)] * 2,
        in_specs=[VMEM] * 8,
        out_specs=[VMEM] * 2,
        compiler_params=params(),
        cost_estimate=COST,
        name="derive",
    )(gate, up, back, *parts, low, rights)


def row_send(x, dz, da, dc):
    pairs = []
    for z in range(4):
        for a in range(2):
            for c in range(2):
                to = ((z + dz) % 4) * 4 + ((a + da) % 2) * 2 + (c + dc) % 2
                pairs.append((z * 4 + a * 2 + c, to))
    return lax.ppermute(x, "row", pairs)


def pair_sum(mine, got):
    return (mine + got.astype(F32)).reshape(4, 2, ROWS, -1)


def z_send(blocks):
    return [row_send(blocks[d].astype(BF), d, 0, 0) for d in (1, 3, 2)]


def z_spread(x):
    return [row_send(x, d, 0, 0) for d in (3, 2, 1)]


def x_send(x):
    return row_send(x.astype(BF), 0, 1, 0)


def core_send(x):
    return row_send(x, 0, 0, 1)


def plus(own, parts):
    for p in parts:
        own = own + p.astype(F32)
    return own


def shards(
    tokens,
    grad_out,
    gate_weight,
    up_weight,
    down_weight,
    gate_left,
    up_left,
    down_left,
    gate_right,
    up_right,
    down_right,
):
    n = gate_weight.shape[1]
    row = lax.axis_index("row")
    z, a, c = row // 4, (row // 2) % 2, row % 2

    k = jnp.arange(2 * HALF, dtype=jnp.int32)
    block = k // ROWS
    dc, dz, da = block // 8, (block // 2) % 4, block % 2
    held = (((z + dz) % 4 * 4) + ((a + da) % 2) * 2 + (c + dc) % 2) * ROWS + k % ROWS
    block = k // ROWS
    dc, dz, da = (block % 2 - c) % 2, (block // 4 - z) % 4, ((block // 2) % 2 - a) % 2
    leave = ((dc * 4 + dz) * 2 + da) * ROWS + k % ROWS
    held, leave = held[:, None], leave[:, None]
    block = (k % RANK) // 8
    dc, dz, da = block // 8, (block // 2) % 4, block % 2
    right_rank = (((z + dz) % 4 * 4) + ((a + da) % 2) * 2 + (c + dc) % 2) * 8 + k % 8 + RANK * (k // RANK)
    left_rank = (k // 48) * 16 + k % 16 + RANK * ((k // 16) % 3)
    match = (left_rank[None, :] == right_rank[:, None]).astype(BF)

    gate_w, up_w, down_w = gate_weight.T, up_weight.T, down_weight.T
    lefts = (gate_left.T, up_left.T, down_left.T)
    edge = jnp.zeros((gate_right.shape[0], -n % 128), BF)
    rights = jnp.concatenate([gate_right, edge, up_right, edge, down_right, edge], axis=1)

    rights_x = x_send(rights)
    held, _ = lax.optimization_barrier((held, rights))
    gate_mine, gate_theirs, tok, out, low = forward_first(tokens, grad_out, held, lefts, gate_w)
    gate = pair_sum(gate_mine, core_send(gate_theirs))
    gate_send = gate[:, 1].astype(BF)
    gate_x = x_send(gate_send)
    rights, rights_x, tok, _, _ = lax.optimization_barrier((rights, rights_x, tok, gate, gate_send))
    rights_pair = jnp.stack([rights, rights_x])
    rights_z = z_spread(rights_pair)
    up_mine, up_theirs = forward(after(tok, rights_pair), up_w)
    up_got = core_send(up_theirs)
    back_mine, back_theirs = forward(after(out, up_theirs), down_w)
    back_got = core_send(back_theirs)
    gate_x, rights_z, _ = lax.optimization_barrier((gate_x, rights_z, back_theirs))
    up = pair_sum(up_mine, up_got)
    up, rights_z, _ = lax.optimization_barrier((up, rights_z, back_theirs))
    up_z = z_send(up)
    back_got, gate_x = lax.optimization_barrier((back_got, gate_x))
    back = pair_sum(back_mine, back_got)
    back_send = back[:, 1].astype(BF)
    back_x = x_send(back_send)

    low, _, _ = lax.optimization_barrier((low, back_send, up))
    low = lax.all_to_all(low, "row", 0, 0, tiled=True).reshape(16, ROWS, RANK)
    low = jnp.sum(low.astype(F32), axis=0)[:, :48].astype(BF).T
    low = jnp.pad(low, ((0, 0), (0, RANK - ROWS)))
    low = jnp.concatenate([jnp.concatenate(lefts, axis=0), low], axis=1)
    low = lax.all_to_all(jnp.broadcast_to(low, (8,) + low.shape), "col", 0, 0, tiled=True)

    gate = gate[:, 0] + gate_x.astype(F32)
    gate, up_z = lax.optimization_barrier((gate, up_z))
    gate_z = z_send(gate)
    up = plus(up[0], up_z)
    up_x = x_send(up[1])
    rights_half = jnp.stack([rights_pair] + rights_z).reshape(64, -1)
    rights_half, up_z = lax.optimization_barrier((rights_half, up_z))
    rights = jnp.concatenate([rights_half, core_send(rights_half)], axis=0)
    low = dot(match, low.reshape(3 * RANK, -1), NN).astype(BF)

    back = back[:, 0] + back_x.astype(F32)
    back, gate_z = lax.optimization_barrier((back, gate_z))
    back_z = z_send(back)
    gate, up, hidden = act(plus(gate[0], gate_z), up[0], up_x, low, rights)
    hidden_x = x_send(hidden)
    gate, hidden_x, back_z = lax.optimization_barrier((gate, hidden_x, back_z))
    hidden = jnp.stack([hidden, hidden_x])
    hidden_z = z_spread(hidden)
    gate_delta, up_delta = derive(gate, up, back[0], back_z, low, rights)
    up_x = x_send(up_delta)
    gate_delta, up_x, hidden_z = lax.optimization_barrier((gate_delta, up_x, hidden_z))
    gate_z = z_spread(gate_delta)

    hidden = jnp.stack([hidden] + hidden_z).reshape(HALF, n)
    hidden = (hidden, core_send(hidden))
    mixed = product(*hidden, down_w, rights, low, 2, index=leave)
    mixed_all = lax.all_to_all(mixed.reshape(8, 48, -1), "col", 0, 0, tiled=True)

    up_delta, gate_z = lax.optimization_barrier((up_delta, gate_z))
    gate_delta = jnp.stack([gate_delta] + gate_z)
    gate_x = x_send(gate_delta)
    up_delta = jnp.stack([up_delta, up_x])
    up_z = z_spread(up_delta)
    hidden, _ = lax.optimization_barrier((hidden, mixed))
    down_grad = weight_grad(*hidden, out)
    up_z, gate_x, mixed_all, _ = lax.optimization_barrier((up_z, gate_x, mixed_all, down_grad))

    up_delta = jnp.stack([up_delta] + up_z).reshape(HALF, n)
    up_delta = (up_delta, core_send(up_delta))
    gate_delta = jnp.stack([gate_delta, gate_x], axis=1).reshape(HALF, n)
    gate_delta = (gate_delta, core_send(gate_delta))
    partial = product(*up_delta, up_w, rights, low, 1)
    input_grad = product(*gate_delta, gate_w, rights, low, 0, partial=partial, index=leave)
    up_delta, gate_delta, _ = lax.optimization_barrier((up_delta, gate_delta, input_grad))
    input_all = lax.all_to_all(input_grad.reshape(8, 48, -1), "col", 0, 0, tiled=True)
    up_grad = weight_grad(*up_delta, tok)
    gate_grad = weight_grad(*gate_delta, tok)
    mixed = jnp.sum(mixed_all.astype(F32), axis=0).astype(BF)
    input_grad = jnp.sum(input_all.astype(F32), axis=0).astype(BF)
    return mixed, input_grad, gate_grad.T, up_grad.T, down_grad.T


def solution(mesh):
    arg = P("row", "col")
    in_specs = (P(None, "row"), P(None, "row")) + (arg,) * 9
    out_specs = (P("col", "row"), P("col", "row")) + (arg,) * 3
    return jax.shard_map(shards, mesh=mesh, in_specs=in_specs, out_specs=out_specs, check_vma=False)
```

```python
import jax
import jax.numpy as jnp
from jax import lax
from jax.experimental import pallas as pl
from jax.experimental.pallas import tpu as pltpu
from jax.sharding import PartitionSpec as P

BF = jnp.bfloat16
F32 = jnp.float32
ROWS = 24
HALF = 192
SIZE = 384
CHUNK = 1408
STEP = 512
RANK = 128

NN = ((1,), (0,))
NT = ((1,), (1,))
TN = ((0,), (0,))

VMEM = pl.BlockSpec(memory_space=pltpu.VMEM)
HBM = pl.BlockSpec(memory_space=pltpu.HBM)


def dot(a, b, dims):
    return lax.dot_general(a, b, (dims, ((), ())), preferred_element_type=F32)


def tie(*arrays):
    return lax.optimization_barrier(arrays)


def cuts(n, step):
    return [(at, min(step, n - at)) for at in range(0, n, step)]


def padded(n):
    return -(-n // 128) * 128


def pick(index_ref, size):
    return (index_ref[...] == lax.broadcasted_iota(jnp.int32, (size, size), 1)).astype(BF)


def pallas(body, name, ins, outs, in_specs, out_specs, scratch):
    return pl.pallas_call(
        body,
        out_shape=outs,
        in_specs=in_specs,
        out_specs=out_specs,
        scratch_shapes=scratch,
        compiler_params=pltpu.CompilerParams(vmem_limit_bytes=16 * 1024 * 1024),
        name=name,
    )(*ins)


def forward_pair(tokens, grad_out, index, gate_w, down_w):
    n, depth = gate_w.shape
    wide = padded(n)

    def body(t_ref, g_ref, i_ref, gw_ref, dw_ref, mine_ref, theirs_ref, tok_ref, out_ref):
        mine_ref[:, n:wide] = jnp.zeros((HALF, wide - n), F32)
        theirs_ref[:, n:wide] = jnp.zeros((HALF, wide - n), BF)
        turn = pick(i_ref, SIZE)

        def product(x_ref, w_ref, first):
            for at, size in cuts(n, CHUNK):
                got = dot(x_ref[...], w_ref[at : at + size, :], NT)
                mine_ref[:, first + at : first + at + size] = got[:HALF]
                theirs_ref[:, first + at : first + at + size] = got[HALF:].astype(BF)

        tok_ref[...] = dot(turn, t_ref[...], NN).astype(BF)
        product(tok_ref, gw_ref, 0)
        out_ref[...] = dot(turn, g_ref[...], NN).astype(BF)
        product(out_ref, dw_ref, wide)

    cols = wide + n
    return pallas(
        body,
        "forward_pair",
        (tokens, grad_out, index, gate_w, down_w),
        [
            jax.ShapeDtypeStruct((HALF, cols), F32),
            jax.ShapeDtypeStruct((HALF, cols), BF),
            jax.ShapeDtypeStruct((SIZE, depth), BF),
            jax.ShapeDtypeStruct((SIZE, depth), BF),
        ],
        [VMEM] * 5,
        [VMEM] * 4,
        [],
    )


def forward_up(tok, out, lefts, up_w):
    n, depth = up_w.shape
    low = 3 * RANK

    def body(t_ref, o_ref, l_ref, w_ref, mine_ref, theirs_ref):
        def put(at, size, got):
            mine_ref[:, at : at + size] = got[:HALF]
            theirs_ref[:, at : at + size] = got[HALF:].astype(BF)

        put(0, 2 * RANK, dot(t_ref[...], l_ref[: 2 * RANK, :], NT))
        put(2 * RANK, RANK, dot(o_ref[...], l_ref[2 * RANK :, :], NT))
        for at, size in cuts(n, CHUNK):
            put(low + at, size, dot(t_ref[...], w_ref[at : at + size, :], NT))

    return pallas(
        body,
        "forward_up",
        (tok, out, lefts, up_w),
        [jax.ShapeDtypeStruct((HALF, low + n), F32), jax.ShapeDtypeStruct((HALF, low + n), BF)],
        [VMEM] * 4,
        [VMEM] * 2,
        [],
    )


def act(pair, pair_x, up, parts, near, far, sort, n):
    wide = padded(n)
    low_n = 3 * RANK

    def body(p_ref, px_ref, u_ref, a_ref, b_ref, c_ref, near_ref, far_ref, sort_ref, hidden_ref, delta_ref):
        def total(at, size):
            part = slice(at, at + size)
            return u_ref[:, part] + a_ref[:, part].astype(F32) + b_ref[:, part].astype(F32) + c_ref[:, part].astype(F32)

        low = total(0, low_n).astype(BF)
        low = [dot(low[:, RANK * t : RANK * (t + 1)], sort_ref[...], NN).astype(BF) for t in range(3)]
        delta_ref[:, n:wide] = jnp.zeros((ROWS, wide - n), BF)
        for at, size in cuts(n, CHUNK):

            def more(t):
                part = slice(wide * t + at, wide * t + at + size)
                return dot(low[t], jnp.concatenate([near_ref[:, part], far_ref[:, part]], axis=0), NN)

            def both(first):
                part = slice(first + at, first + at + size)
                return p_ref[:, part] + px_ref[:, part].astype(F32)

            gate = both(0) + more(0)
            up_value = total(low_n + at, size) + more(1)
            back = both(wide) + more(2)
            sigma = jax.nn.sigmoid(gate)
            hidden_ref[:, at : at + size] = (gate * sigma * up_value).astype(BF)
            slope = sigma * (1.0 + gate * (1.0 - sigma))
            delta_ref[:, at : at + size] = (back * up_value * slope).astype(BF)
            delta_ref[:, wide + at : wide + at + size] = (back * gate * sigma).astype(BF)

    return pallas(
        body,
        "act",
        (pair, pair_x, up, *parts, near, far, sort),
        [jax.ShapeDtypeStruct((ROWS, n), BF), jax.ShapeDtypeStruct((ROWS, wide + n), BF)],
        [VMEM] * 9,
        [VMEM] * 2,
        [],
    )


def through(mine_ref, other_ref, first, w_ref, near_ref, far_ref, left_ref, sort_ref, place):
    n = w_ref.shape[0]
    wide = padded(n)
    total = low = None
    for at, size in cuts(n, CHUNK):
        part = slice(first + at, first + at + size)
        value = jnp.concatenate([mine_ref[:, part], other_ref[:, part]], axis=0)
        part = slice(wide * place + at, wide * place + at + size)
        right = jnp.concatenate([near_ref[:, part], far_ref[:, part]], axis=0)
        more = dot(value, right, NT)
        low = more if low is None else low + more
        more = dot(value, w_ref[at : at + size, :], NN)
        total = more if total is None else total + more
    low = dot(low.astype(BF), sort_ref[...], NT).astype(BF)
    return total + dot(low, left_ref[RANK * place : RANK * (place + 1), :], NN)


def grads(mine_ref, other_ref, first, x_ref, grad_ref, grad_hbm, sems, slot=0):
    n = grad_ref.shape[0]
    sent = []
    for k, (at, size) in enumerate(cuts(n, STEP)):
        part = slice(first + at, first + at + size)
        value = jnp.concatenate([mine_ref[:, part], other_ref[:, part]], axis=0)
        grad_ref[at : at + size, :] = dot(value, x_ref[...], TN).astype(BF)
        part = pl.ds(at, size)
        sent.append(pltpu.make_async_copy(grad_ref.at[part, :], grad_hbm.at[part, :], sems.at[slot + k]))
        sent[-1].start()
    return sent


def backward_hidden(mine, other, x, weight, near, far, lefts, sort, index):
    n, depth = weight.shape

    def body(m_ref, o_ref, x_ref, near_ref, far_ref, l_ref, s_ref, i_ref, w_ref, out_ref, grad_hbm, grad_ref, sems):
        sent = grads(m_ref, o_ref, 0, x_ref, grad_ref, grad_hbm, sems)
        total = through(m_ref, o_ref, 0, w_ref, near_ref, far_ref, l_ref, s_ref, 2)
        out_ref[...] = dot(pick(i_ref, SIZE), total.astype(BF), NN).astype(BF)
        for copy in sent:
            copy.wait()

    return pallas(
        body,
        "backward_hidden",
        (mine, other, x, near, far, lefts, sort, index, weight),
        [jax.ShapeDtypeStruct((SIZE, depth), BF), jax.ShapeDtypeStruct((n, depth), BF)],
        [VMEM] * 9,
        [VMEM, HBM],
        [pltpu.VMEM((n, depth), BF), pltpu.SemaphoreType.DMA((len(cuts(n, STEP)),))],
    )


def backward_pair(mine, other, gate_w, up_w, near, far, lefts, sort, index):
    n, depth = gate_w.shape
    wide = padded(n)

    def body(m_ref, o_ref, near_ref, far_ref, l_ref, s_ref, i_ref, gw_ref, uw_ref, out_ref):
        total = through(m_ref, o_ref, 0, gw_ref, near_ref, far_ref, l_ref, s_ref, 0)
        total = total + through(m_ref, o_ref, wide, uw_ref, near_ref, far_ref, l_ref, s_ref, 1)
        out_ref[...] = dot(pick(i_ref, SIZE), total.astype(BF), NN).astype(BF)

    return pallas(
        body,
        "backward_pair",
        (mine, other, near, far, lefts, sort, index, gate_w, up_w),
        jax.ShapeDtypeStruct((SIZE, depth), BF),
        [VMEM] * 9,
        VMEM,
        [],
    )


def weight_grad(mine, other, x, first, n):
    depth = x.shape[1]

    def body(m_ref, o_ref, x_ref, grad_hbm, grad_ref, sems):
        for copy in grads(m_ref, o_ref, first, x_ref, grad_ref, grad_hbm, sems):
            copy.wait()

    return pallas(
        body,
        "weight_grad",
        (mine, other, x),
        jax.ShapeDtypeStruct((n, depth), BF),
        [VMEM] * 3,
        HBM,
        [pltpu.VMEM((n, depth), BF), pltpu.SemaphoreType.DMA((len(cuts(n, STEP)),))],
    )


def row_send(x, dz, da, dc):
    pairs = []
    for z in range(4):
        for a in range(2):
            for c in range(2):
                to = ((z + dz) % 4) * 4 + ((a + da) % 2) * 2 + (c + dc) % 2
                pairs.append((z * 4 + a * 2 + c, to))
    return lax.ppermute(x, "row", pairs)


def col_send(x, dh, dy):
    pairs = []
    for h in range(2):
        for y in range(4):
            pairs.append((h * 4 + y, ((h + dh) % 2) * 4 + (y + dy) % 4))
    return lax.ppermute(x, "col", pairs)


def z_send(blocks):
    return [row_send(blocks[d].astype(BF), d, 0, 0) for d in (1, 3, 2)]


def z_spread(x):
    return [row_send(x, d, 0, 0) for d in (3, 2, 1)]


def x_send(x):
    return row_send(x, 0, 1, 0)


def core_send(x):
    return row_send(x, 0, 0, 1)


def pair_sum(mine, got):
    return (mine + got.astype(F32)).reshape(4, 2, ROWS, -1)


def plus(own, parts):
    for p in parts:
        own = own + p.astype(F32)
    return own


def shards(
    tokens,
    grad_out,
    gate_weight,
    up_weight,
    down_weight,
    gate_left,
    up_left,
    down_left,
    gate_right,
    up_right,
    down_right,
):
    n = gate_weight.shape[1]
    row, col = lax.axis_index("row"), lax.axis_index("col")
    z, a, c = row // 4, (row // 2) % 2, row % 2
    h, y = col // 4, col % 4

    k = jnp.arange(SIZE, dtype=jnp.int32)

    def owner(block):
        dc, dz, da = block // 8, (block // 2) % 4, block % 2
        return (z + dz) % 4 * 4 + (a + da) % 2 * 2 + (c + dc) % 2

    held = owner(k // ROWS) * ROWS + k % ROWS
    dest = (((h + k // 192) % 2) * 4 + (y + k // 48) % 4) * 48 + k % 48
    block = dest // ROWS
    dc, dz, da = (block % 2 - c) % 2, (block // 4 - z) % 4, ((block // 2) % 2 - a) % 2
    leave = ((dc * 4 + dz) * 2 + da) * ROWS + dest % ROWS
    held, leave = held[:, None], leave[:, None]
    j = jnp.arange(RANK, dtype=jnp.int32)
    sort = (j[:, None] == (owner(j // 8) * 8 + j % 8)[None, :]).astype(BF)
    my, mh, mt, mi = k // 96, (k // 48) % 2, (k // 16) % 3, k % 16
    rank = (((h - mh) % 2) * 4 + (y - my) % 4) * 16 + mi + RANK * mt
    match = (rank[None, :] == k[:, None]).astype(BF)

    gate_w, up_w, down_w = gate_weight.T, up_weight.T, down_weight.T
    edge = jnp.zeros((gate_right.shape[0], padded(n) - n), BF)
    rights = jnp.concatenate([gate_right, edge, up_right, edge, down_right, edge], axis=1)
    lefts = jnp.concatenate([gate_left.T, up_left.T, down_left.T], axis=0)
    lefts_h = col_send(lefts, 1, 0)
    rights_z = z_spread(rights)
    held, rights, lefts = tie(held, rights, lefts)

    mine, theirs, tok, out = forward_pair(tokens, grad_out, held, gate_w, down_w)
    got = core_send(theirs)
    lefts_h, tok = tie(lefts_h, tok)
    lefts = jnp.stack([lefts, lefts_h])
    lefts_y = [col_send(lefts, 0, d) for d in (1, 2, 3)]
    rights = jnp.stack([rights] + rights_z)
    rights_x = x_send(rights)

    tok, pair = tie(tok, pair_sum(mine, got))
    pair_z = z_send(pair)
    lefts = jnp.stack([lefts] + lefts_y).reshape(SIZE, -1)
    lefts = dot(match, lefts, NN).astype(BF)
    mine, theirs = forward_up(tok, out, lefts, up_w)
    got, rights_x = tie(core_send(theirs), rights_x)
    up = pair_sum(mine, got)
    up_x = x_send(up[:, 1].astype(BF))
    near = jnp.stack([rights, rights_x], axis=1).reshape(64, -1)
    far = core_send(near)

    *pair_z, up_x = tie(*pair_z, up_x)
    pair = plus(pair[0], pair_z)
    pair_x = x_send(pair[1].astype(BF))
    up = up[:, 0] + up_x.astype(F32)
    up_z = z_send(up)
    hidden, delta = act(pair[0], pair_x, up[0], up_z, near, far, sort, n)

    delta_x = x_send(delta)
    hidden_z = z_spread(hidden)
    delta_x, hidden_z = tie(delta_x, hidden_z)
    delta = jnp.stack([delta, delta_x])
    delta_z = z_spread(delta)
    hidden = jnp.stack([hidden] + hidden_z)
    hidden_x, delta_z = tie(x_send(hidden), delta_z)
    hidden = jnp.stack([hidden, hidden_x], axis=1).reshape(HALF, n)
    hidden_far = core_send(hidden)
    mixed, down_grad = backward_hidden(hidden, hidden_far, out, down_w, near, far, lefts, sort, leave)
    delta = jnp.stack([delta] + delta_z).reshape(HALF, -1)
    delta_far, mixed = tie(core_send(delta), mixed)
    input_grad = backward_pair(delta, delta_far, gate_w, up_w, near, far, lefts, sort, leave)

    both = jnp.stack([mixed, input_grad]).reshape(2, 2, 4, 48, -1)
    leaving = both[:, 1]
    delta, leaving = tie(delta, leaving)
    both_h = col_send(leaving, 1, 0)
    up_grad = weight_grad(delta, delta_far, tok, padded(n), n)
    both_h, delta, up_grad = tie(both_h, delta, up_grad)
    both = both[:, 0].astype(F32) + both_h.astype(F32)
    delta, leaving = tie(delta, both[:, 1:].astype(BF))
    both_y = [col_send(leaving[:, d - 1], 0, d) for d in (1, 3, 2)]
    gate_grad = weight_grad(delta, delta_far, tok, 0, n)
    both = plus(both[:, 0], both_y).astype(BF)
    return both[0], both[1], gate_grad.T, up_grad.T, down_grad.T


def solution(mesh):
    arg = P("row", "col")
    in_specs = (P(None, "row"), P(None, "row")) + (arg,) * 9
    out_specs = (P("col", "row"), P("col", "row")) + (arg,) * 3
    return jax.shard_map(shards, mesh=mesh, in_specs=in_specs, out_specs=out_specs, check_vma=False)
```

```python
import jax
import jax.numpy as jnp
from jax import lax
from jax.experimental import pallas as pl
from jax.experimental.pallas import tpu as pltpu
from jax.sharding import PartitionSpec as P

BF = jnp.bfloat16
F32 = jnp.float32
ROWS = 24
HALF = 192
SIZE = 384
CHUNK = 1408
STEP = 512
RANK = 128

NN = ((1,), (0,))
NT = ((1,), (1,))
TN = ((0,), (0,))

VMEM = pl.BlockSpec(memory_space=pltpu.VMEM)
HBM = pl.BlockSpec(memory_space=pltpu.HBM)


def dot(a, b, dims):
    return lax.dot_general(a, b, (dims, ((), ())), preferred_element_type=F32)


def tie(*arrays):
    return lax.optimization_barrier(arrays)


def cuts(n, step):
    return [(at, min(step, n - at)) for at in range(0, n, step)]


def padded(n):
    return -(-n // 128) * 128


def pick(index_ref, size):
    return (index_ref[...] == lax.broadcasted_iota(jnp.int32, (size, size), 1)).astype(BF)


def pallas(body, name, ins, outs, in_specs, out_specs, scratch):
    return pl.pallas_call(
        body,
        out_shape=outs,
        in_specs=in_specs,
        out_specs=out_specs,
        scratch_shapes=scratch,
        compiler_params=pltpu.CompilerParams(vmem_limit_bytes=16 * 1024 * 1024),
        name=name,
    )(*ins)


def forward_theirs(tokens, grad_out, index, gate_w, down_w):
    n, depth = gate_w.shape
    wide = padded(n)

    def body(t_ref, g_ref, i_ref, gw_ref, dw_ref, theirs_ref, tok_ref, out_ref):
        theirs_ref[:, n:wide] = jnp.zeros((HALF, wide - n), BF)
        turn = pick(i_ref, SIZE)
        for in_ref, turned_ref, w_ref, first in ((t_ref, tok_ref, gw_ref, 0), (g_ref, out_ref, dw_ref, wide)):
            turned_ref[...] = dot(turn, in_ref[...], NN).astype(BF)
            for at, size in cuts(n, CHUNK):
                got = dot(turned_ref[HALF:, :], w_ref[at : at + size, :], NT)
                theirs_ref[:, first + at : first + at + size] = got.astype(BF)

    return pallas(
        body,
        "forward_theirs",
        (tokens, grad_out, index, gate_w, down_w),
        [jax.ShapeDtypeStruct((HALF, wide + n), BF)] + [jax.ShapeDtypeStruct((SIZE, depth), BF)] * 2,
        [VMEM] * 5,
        [VMEM] * 3,
        [],
    )


def forward_mine(tok, out, gate_w, down_w, got):
    n, depth = gate_w.shape
    wide = padded(n)
    quarter = HALF // 4

    def body(t_ref, o_ref, gw_ref, dw_ref, got_ref, own_ref, *send_refs):
        own_ref[:, n:wide] = jnp.zeros((quarter, wide - n), F32)
        for ref in send_refs:
            ref[:, n:wide] = jnp.zeros((quarter, wide - n), BF)
        for x_ref, w_ref, first in ((t_ref, gw_ref, 0), (o_ref, dw_ref, wide)):
            for at, size in cuts(n, CHUNK):
                part = slice(first + at, first + at + size)
                total = dot(x_ref[:HALF, :], w_ref[at : at + size, :], NT) + got_ref[:, part].astype(F32)
                own_ref[:, part] = total[:quarter]
                for d, ref in enumerate(send_refs, 1):
                    ref[:, part] = total[quarter * d : quarter * (d + 1)].astype(BF)

    return pallas(
        body,
        "forward_mine",
        (tok, out, gate_w, down_w, got),
        [jax.ShapeDtypeStruct((quarter, wide + n), F32)] + [jax.ShapeDtypeStruct((quarter, wide + n), BF)] * 3,
        [VMEM] * 5,
        [VMEM] * 4,
        [],
    )


def forward_up(tok, out, lefts, up_w):
    n, depth = up_w.shape
    low = 3 * RANK

    def body(t_ref, o_ref, l_ref, w_ref, mine_ref, theirs_ref):
        def put(at, size, got):
            mine_ref[:, at : at + size] = got[:HALF]
            theirs_ref[:, at : at + size] = got[HALF:].astype(BF)

        put(0, 2 * RANK, dot(t_ref[...], l_ref[: 2 * RANK, :], NT))
        put(2 * RANK, RANK, dot(o_ref[...], l_ref[2 * RANK :, :], NT))
        for at, size in cuts(n, CHUNK):
            put(low + at, size, dot(t_ref[...], w_ref[at : at + size, :], NT))

    return pallas(
        body,
        "forward_up",
        (tok, out, lefts, up_w),
        [jax.ShapeDtypeStruct((HALF, low + n), F32), jax.ShapeDtypeStruct((HALF, low + n), BF)],
        [VMEM] * 4,
        [VMEM] * 2,
        [],
    )


def act(pair, pair_x, up, parts, near, far, sort, n):
    wide = padded(n)
    low_n = 3 * RANK

    def body(p_ref, px_ref, u_ref, a_ref, b_ref, c_ref, near_ref, far_ref, sort_ref, hidden_ref, delta_ref):
        def total(at, size):
            part = slice(at, at + size)
            return u_ref[:, part] + a_ref[:, part].astype(F32) + b_ref[:, part].astype(F32) + c_ref[:, part].astype(F32)

        low = total(0, low_n).astype(BF)
        low = [dot(low[:, RANK * t : RANK * (t + 1)], sort_ref[...], NN).astype(BF) for t in range(3)]
        delta_ref[:, n:wide] = jnp.zeros((ROWS, wide - n), BF)
        for at, size in cuts(n, CHUNK):

            def more(t):
                part = slice(wide * t + at, wide * t + at + size)
                return dot(low[t], jnp.concatenate([near_ref[:, part], far_ref[:, part]], axis=0), NN)

            def both(first):
                part = slice(first + at, first + at + size)
                return p_ref[:, part] + px_ref[:, part].astype(F32)

            gate = both(0) + more(0)
            up_value = total(low_n + at, size) + more(1)
            back = both(wide) + more(2)
            sigma = jax.nn.sigmoid(gate)
            hidden_ref[:, at : at + size] = (gate * sigma * up_value).astype(BF)
            slope = sigma * (1.0 + gate * (1.0 - sigma))
            delta_ref[:, at : at + size] = (back * up_value * slope).astype(BF)
            delta_ref[:, wide + at : wide + at + size] = (back * gate * sigma).astype(BF)

    return pallas(
        body,
        "act",
        (pair, pair_x, up, *parts, near, far, sort),
        [jax.ShapeDtypeStruct((ROWS, n), BF), jax.ShapeDtypeStruct((ROWS, wide + n), BF)],
        [VMEM] * 9,
        [VMEM] * 2,
        [],
    )


def through(mine_ref, other_ref, first, w_ref, near_ref, far_ref, left_ref, sort_ref, place):
    n = w_ref.shape[0]
    wide = padded(n)
    total = low = None
    for at, size in cuts(n, CHUNK):
        part = slice(first + at, first + at + size)
        value = jnp.concatenate([mine_ref[:, part], other_ref[:, part]], axis=0)
        part = slice(wide * place + at, wide * place + at + size)
        right = jnp.concatenate([near_ref[:, part], far_ref[:, part]], axis=0)
        more = dot(value, right, NT)
        low = more if low is None else low + more
        more = dot(value, w_ref[at : at + size, :], NN)
        total = more if total is None else total + more
    low = dot(low.astype(BF), sort_ref[...], NT).astype(BF)
    return total + dot(low, left_ref[RANK * place : RANK * (place + 1), :], NN)


def grads(mine_ref, other_ref, first, x_ref, grad_ref, grad_hbm, sems, slot=0):
    n = grad_ref.shape[0]
    sent = []
    for k, (at, size) in enumerate(cuts(n, STEP)):
        part = slice(first + at, first + at + size)
        value = jnp.concatenate([mine_ref[:, part], other_ref[:, part]], axis=0)
        grad_ref[at : at + size, :] = dot(value, x_ref[...], TN).astype(BF)
        part = pl.ds(at, size)
        sent.append(pltpu.make_async_copy(grad_ref.at[part, :], grad_hbm.at[part, :], sems.at[slot + k]))
        sent[-1].start()
    return sent


def backward_hidden(mine, other, x, weight, near, far, lefts, sort, index):
    n, depth = weight.shape

    def body(m_ref, o_ref, x_ref, near_ref, far_ref, l_ref, s_ref, i_ref, w_ref, out_ref, grad_hbm, grad_ref, sems):
        sent = grads(m_ref, o_ref, 0, x_ref, grad_ref, grad_hbm, sems)
        total = through(m_ref, o_ref, 0, w_ref, near_ref, far_ref, l_ref, s_ref, 2)
        out_ref[...] = dot(pick(i_ref, SIZE), total.astype(BF), NN).astype(BF)
        for copy in sent:
            copy.wait()

    return pallas(
        body,
        "backward_hidden",
        (mine, other, x, near, far, lefts, sort, index, weight),
        [jax.ShapeDtypeStruct((SIZE, depth), BF), jax.ShapeDtypeStruct((n, depth), BF)],
        [VMEM] * 9,
        [VMEM, HBM],
        [pltpu.VMEM((n, depth), BF), pltpu.SemaphoreType.DMA((len(cuts(n, STEP)),))],
    )


def backward_pair(mine, other, gate_w, up_w, near, far, lefts, sort, index):
    n, depth = gate_w.shape
    wide = padded(n)

    def body(m_ref, o_ref, near_ref, far_ref, l_ref, s_ref, i_ref, gw_ref, uw_ref, out_ref):
        total = through(m_ref, o_ref, 0, gw_ref, near_ref, far_ref, l_ref, s_ref, 0)
        total = total + through(m_ref, o_ref, wide, uw_ref, near_ref, far_ref, l_ref, s_ref, 1)
        out_ref[...] = dot(pick(i_ref, SIZE), total.astype(BF), NN).astype(BF)

    return pallas(
        body,
        "backward_pair",
        (mine, other, near, far, lefts, sort, index, gate_w, up_w),
        jax.ShapeDtypeStruct((SIZE, depth), BF),
        [VMEM] * 9,
        VMEM,
        [],
    )


def weight_grad(mine, other, x, first, n):
    depth = x.shape[1]

    def body(m_ref, o_ref, x_ref, grad_hbm, grad_ref, sems):
        for copy in grads(m_ref, o_ref, first, x_ref, grad_ref, grad_hbm, sems):
            copy.wait()

    return pallas(
        body,
        "weight_grad",
        (mine, other, x),
        jax.ShapeDtypeStruct((n, depth), BF),
        [VMEM] * 3,
        HBM,
        [pltpu.VMEM((n, depth), BF), pltpu.SemaphoreType.DMA((len(cuts(n, STEP)),))],
    )


def row_send(x, dz, da, dc):
    pairs = []
    for z in range(4):
        for a in range(2):
            for c in range(2):
                to = ((z + dz) % 4) * 4 + ((a + da) % 2) * 2 + (c + dc) % 2
                pairs.append((z * 4 + a * 2 + c, to))
    return lax.ppermute(x, "row", pairs)


def col_send(x, dh, dy):
    pairs = []
    for h in range(2):
        for y in range(4):
            pairs.append((h * 4 + y, ((h + dh) % 2) * 4 + (y + dy) % 4))
    return lax.ppermute(x, "col", pairs)


def z_send(blocks):
    return [row_send(blocks[d].astype(BF), d, 0, 0) for d in (1, 3, 2)]


def z_spread(x):
    return [row_send(x, d, 0, 0) for d in (3, 2, 1)]


def x_send(x):
    return row_send(x, 0, 1, 0)


def core_send(x):
    return row_send(x, 0, 0, 1)


def pair_sum(mine, got):
    return (mine + got.astype(F32)).reshape(4, 2, ROWS, -1)


def plus(own, parts):
    for p in parts:
        own = own + p.astype(F32)
    return own


def shards(
    tokens,
    grad_out,
    gate_weight,
    up_weight,
    down_weight,
    gate_left,
    up_left,
    down_left,
    gate_right,
    up_right,
    down_right,
):
    n = gate_weight.shape[1]
    row, col = lax.axis_index("row"), lax.axis_index("col")
    z, a, c = row // 4, (row // 2) % 2, row % 2
    h, y = col // 4, col % 4
    z, a, c, h, y, tokens, grad_out, gate_weight, down_weight, *small = tie(
        *(z, a, c, h, y, tokens, grad_out, gate_weight, down_weight),
        *(gate_left, up_left, down_left, gate_right, up_right, down_right),
    )
    gate_left, up_left, down_left, gate_right, up_right, down_right = small

    k = jnp.arange(SIZE, dtype=jnp.int32)

    def owner(block):
        dc, dz, da = block // 8, (block // 2) % 4, block % 2
        return (z + dz) % 4 * 4 + (a + da) % 2 * 2 + (c + dc) % 2

    held = owner(k // ROWS) * ROWS + k % ROWS
    dest = (((h + k // 192) % 2) * 4 + (y + k // 48) % 4) * 48 + k % 48
    block = dest // ROWS
    dc, dz, da = (block % 2 - c) % 2, (block // 4 - z) % 4, ((block // 2) % 2 - a) % 2
    leave = ((dc * 4 + dz) * 2 + da) * ROWS + dest % ROWS
    held, leave = held[:, None], leave[:, None]
    j = jnp.arange(RANK, dtype=jnp.int32)
    sort = (j[:, None] == (owner(j // 8) * 8 + j % 8)[None, :]).astype(BF)
    my, mh, mt, mi = k // 96, (k // 48) % 2, (k // 16) % 3, k % 16
    rank = (((h - mh) % 2) * 4 + (y - my) % 4) * 16 + mi + RANK * mt
    match = (rank[None, :] == k[:, None]).astype(BF)

    gate_w, up_w, down_w = gate_weight.T, up_weight.T, down_weight.T
    edge = jnp.zeros((gate_right.shape[0], padded(n) - n), BF)
    rights = jnp.concatenate([gate_right, edge, up_right, edge, down_right, edge], axis=1)
    lefts = jnp.concatenate([gate_left.T, up_left.T, down_left.T], axis=0)
    lefts_h = col_send(lefts, 1, 0)
    rights_z = z_spread(rights)
    held, leave, sort, match, rights, lefts, lefts_h, *rights_z = tie(
        held, leave, sort, match, rights, lefts, lefts_h, *rights_z
    )

    theirs, tok, out = forward_theirs(tokens, grad_out, held, gate_w, down_w)
    got = core_send(theirs)
    lefts = jnp.stack([lefts, lefts_h])
    lefts_y = [col_send(lefts, 0, d) for d in (1, 2, 3)]
    rights = jnp.stack([rights] + rights_z)
    rights_x = x_send(rights)

    pair, *sends = forward_mine(tok, out, gate_w, down_w, got)
    tok, pair = tie(tok, pair)
    pair_z = [row_send(sends[d - 1], d, 0, 0) for d in (1, 3, 2)]
    lefts = jnp.stack([lefts] + lefts_y).reshape(SIZE, -1)
    lefts = dot(match, lefts, NN).astype(BF)
    mine, theirs = forward_up(tok, out, lefts, up_w)
    got, rights_x = tie(core_send(theirs), rights_x)
    up = pair_sum(mine, got)
    up_x = x_send(up[:, 1].astype(BF))
    near = jnp.stack([rights, rights_x], axis=1).reshape(64, -1)
    far = core_send(near)

    *pair_z, up_x = tie(*pair_z, up_x)
    pair = plus(pair, pair_z).reshape(2, ROWS, -1)
    pair_x = x_send(pair[1].astype(BF))
    up = up[:, 0] + up_x.astype(F32)
    up_z = z_send(up)
    hidden, delta = act(pair[0], pair_x, up[0], up_z, near, far, sort, n)

    delta_x = x_send(delta)
    hidden_z = z_spread(hidden)
    delta_x, hidden_z = tie(delta_x, hidden_z)
    delta = jnp.stack([delta, delta_x])
    delta_z = z_spread(delta)
    hidden = jnp.stack([hidden] + hidden_z)
    hidden_x, delta_z = tie(x_send(hidden), delta_z)
    hidden = jnp.stack([hidden, hidden_x], axis=1).reshape(HALF, n)
    delta = jnp.stack([delta] + delta_z).reshape(HALF, -1)
    hidden_far, delta = tie(core_send(hidden), delta)
    delta_far = core_send(delta)
    mixed, down_grad = backward_hidden(hidden, hidden_far, out, down_w, near, far, lefts, sort, leave)
    mixed = mixed.reshape(2, 4, 48, -1)
    mixed_h = col_send(mixed[1], 1, 0)
    delta_far, mixed = tie(delta_far, mixed)
    input_grad = backward_pair(delta, delta_far, gate_w, up_w, near, far, lefts, sort, leave)
    input_grad = input_grad.reshape(2, 4, 48, -1)
    delta, leaving = tie(delta, input_grad[1])
    input_h = col_send(leaving, 1, 0)
    up_grad = weight_grad(delta, delta_far, tok, padded(n), n)
    input_h, delta, up_grad = tie(input_h, delta, up_grad)
    both = [mixed[0].astype(F32) + mixed_h.astype(F32), input_grad[0].astype(F32) + input_h.astype(F32)]
    leaving = [jnp.stack([part[d] for part in both]).astype(BF) for d in (1, 3, 2)]
    delta, *leaving = tie(delta, *leaving)
    both_y = [col_send(part, 0, d) for part, d in zip(leaving, (1, 3, 2))]
    gate_grad = weight_grad(delta, delta_far, tok, 0, n)
    both = [plus(both[t][0], [part[t] for part in both_y]).astype(BF) for t in range(2)]
    return both[0], both[1], gate_grad.T, up_grad.T, down_grad.T


def solution(mesh):
    arg = P("row", "col")
    in_specs = (P(None, "row"), P(None, "row")) + (arg,) * 9
    out_specs = (P("col", "row"), P("col", "row")) + (arg,) * 3
    return jax.shard_map(shards, mesh=mesh, in_specs=in_specs, out_specs=out_specs, check_vma=False)
```

```python
import jax
import jax.numpy as jnp
from jax import lax
from jax.experimental import pallas as pl
from jax.experimental.pallas import tpu as pltpu
from jax.sharding import PartitionSpec as P

BF = jnp.bfloat16
F32 = jnp.float32
ROWS = 24
HALF = 192
SIZE = 384
CHUNK = 1408
STEP = 512
RANK = 128

NN = ((1,), (0,))
NT = ((1,), (1,))
TN = ((0,), (0,))

VMEM = pl.BlockSpec(memory_space=pltpu.VMEM)
HBM = pl.BlockSpec(memory_space=pltpu.HBM)


def dot(a, b, dims):
    return lax.dot_general(a, b, (dims, ((), ())), preferred_element_type=F32)


def tie(*arrays):
    return lax.optimization_barrier(arrays)


def cuts(n, step):
    return [(at, min(step, n - at)) for at in range(0, n, step)]


def padded(n):
    return -(-n // 128) * 128


def pick(index_ref, size):
    return (index_ref[...] == lax.broadcasted_iota(jnp.int32, (size, size), 1)).astype(BF)


def pallas(body, name, ins, outs, in_specs, out_specs, scratch):
    return pl.pallas_call(
        body,
        out_shape=outs,
        in_specs=in_specs,
        out_specs=out_specs,
        scratch_shapes=scratch,
        compiler_params=pltpu.CompilerParams(vmem_limit_bytes=16 * 1024 * 1024),
        name=name,
    )(*ins)


def forward_theirs(tokens, grad_out, index, gate_w, down_w):
    n, depth = gate_w.shape
    wide = padded(n)

    def body(t_ref, g_ref, i_ref, gw_ref, dw_ref, theirs_ref, tok_ref, out_ref):
        theirs_ref[:, n:wide] = jnp.zeros((HALF, wide - n), BF)
        turn = pick(i_ref, SIZE)
        for in_ref, turned_ref, w_ref, first in ((t_ref, tok_ref, gw_ref, 0), (g_ref, out_ref, dw_ref, wide)):
            turned_ref[...] = dot(turn, in_ref[...], NN).astype(BF)
            for at, size in cuts(n, CHUNK):
                got = dot(turned_ref[HALF:, :], w_ref[at : at + size, :], NT)
                theirs_ref[:, first + at : first + at + size] = got.astype(BF)

    return pallas(
        body,
        "forward_theirs",
        (tokens, grad_out, index, gate_w, down_w),
        [jax.ShapeDtypeStruct((HALF, wide + n), BF)] + [jax.ShapeDtypeStruct((SIZE, depth), BF)] * 2,
        [VMEM] * 5,
        [VMEM] * 3,
        [],
    )


def forward_mine(tok, out, gate_w, down_w, got):
    n, depth = gate_w.shape
    wide = padded(n)
    quarter = HALF // 4

    def body(t_ref, o_ref, gw_ref, dw_ref, got_ref, own_ref, *send_refs):
        own_ref[:, n:wide] = jnp.zeros((quarter, wide - n), F32)
        for ref in send_refs:
            ref[:, n:wide] = jnp.zeros((quarter, wide - n), BF)
        for x_ref, w_ref, first in ((t_ref, gw_ref, 0), (o_ref, dw_ref, wide)):
            for at, size in cuts(n, CHUNK):
                part = slice(first + at, first + at + size)
                total = dot(x_ref[:HALF, :], w_ref[at : at + size, :], NT) + got_ref[:, part].astype(F32)
                own_ref[:, part] = total[:quarter]
                for d, ref in enumerate(send_refs, 1):
                    ref[:, part] = total[quarter * d : quarter * (d + 1)].astype(BF)

    return pallas(
        body,
        "forward_mine",
        (tok, out, gate_w, down_w, got),
        [jax.ShapeDtypeStruct((quarter, wide + n), F32)] + [jax.ShapeDtypeStruct((quarter, wide + n), BF)] * 3,
        [VMEM] * 5,
        [VMEM] * 4,
        [],
    )


def forward_up(tok, out, lefts, up_w):
    n, depth = up_w.shape
    low = 3 * RANK

    def body(t_ref, o_ref, l_ref, w_ref, mine_ref, theirs_ref):
        def put(at, size, got):
            mine_ref[:, at : at + size] = got[:HALF]
            theirs_ref[:, at : at + size] = got[HALF:].astype(BF)

        put(0, 2 * RANK, dot(t_ref[...], l_ref[: 2 * RANK, :], NT))
        put(2 * RANK, RANK, dot(o_ref[...], l_ref[2 * RANK :, :], NT))
        for at, size in cuts(n, CHUNK):
            put(low + at, size, dot(t_ref[...], w_ref[at : at + size, :], NT))

    return pallas(
        body,
        "forward_up",
        (tok, out, lefts, up_w),
        [jax.ShapeDtypeStruct((HALF, low + n), F32), jax.ShapeDtypeStruct((HALF, low + n), BF)],
        [VMEM] * 4,
        [VMEM] * 2,
        [],
    )


def act(pair, pair_x, up, parts, near, far, sort, n):
    wide = padded(n)
    low_n = 3 * RANK

    def body(p_ref, px_ref, u_ref, a_ref, b_ref, c_ref, near_ref, far_ref, sort_ref, hidden_ref, delta_ref):
        def total(at, size):
            part = slice(at, at + size)
            return u_ref[:, part] + a_ref[:, part].astype(F32) + b_ref[:, part].astype(F32) + c_ref[:, part].astype(F32)

        low = total(0, low_n).astype(BF)
        low = [dot(low[:, RANK * t : RANK * (t + 1)], sort_ref[...], NN).astype(BF) for t in range(3)]
        delta_ref[:, n:wide] = jnp.zeros((ROWS, wide - n), BF)
        for at, size in cuts(n, CHUNK):

            def more(t):
                part = slice(wide * t + at, wide * t + at + size)
                return dot(low[t], jnp.concatenate([near_ref[:, part], far_ref[:, part]], axis=0), NN)

            def both(first):
                part = slice(first + at, first + at + size)
                return p_ref[:, part] + px_ref[:, part].astype(F32)

            gate = both(0) + more(0)
            up_value = total(low_n + at, size) + more(1)
            back = both(wide) + more(2)
            sigma = jax.nn.sigmoid(gate)
            hidden_ref[:, at : at + size] = (gate * sigma * up_value).astype(BF)
            slope = sigma * (1.0 + gate * (1.0 - sigma))
            delta_ref[:, at : at + size] = (back * up_value * slope).astype(BF)
            delta_ref[:, wide + at : wide + at + size] = (back * gate * sigma).astype(BF)

    return pallas(
        body,
        "act",
        (pair, pair_x, up, *parts, near, far, sort),
        [jax.ShapeDtypeStruct((ROWS, n), BF), jax.ShapeDtypeStruct((ROWS, wide + n), BF)],
        [VMEM] * 9,
        [VMEM] * 2,
        [],
    )


def through(mine_ref, other_ref, first, w_ref, near_ref, far_ref, left_ref, sort_ref, place):
    n = w_ref.shape[0]
    wide = padded(n)
    total = low = None
    for at, size in cuts(n, CHUNK):
        part = slice(first + at, first + at + size)
        value = jnp.concatenate([mine_ref[:, part], other_ref[:, part]], axis=0)
        part = slice(wide * place + at, wide * place + at + size)
        right = jnp.concatenate([near_ref[:, part], far_ref[:, part]], axis=0)
        more = dot(value, right, NT)
        low = more if low is None else low + more
        more = dot(value, w_ref[at : at + size, :], NN)
        total = more if total is None else total + more
    low = dot(low.astype(BF), sort_ref[...], NT).astype(BF)
    return total + dot(low, left_ref[RANK * place : RANK * (place + 1), :], NN)


def grads(mine_ref, other_ref, first, x_ref, grad_ref, grad_hbm, sems, slot=0):
    n = grad_ref.shape[0]
    sent = []
    for k, (at, size) in enumerate(cuts(n, STEP)):
        part = slice(first + at, first + at + size)
        value = jnp.concatenate([mine_ref[:, part], other_ref[:, part]], axis=0)
        grad_ref[at : at + size, :] = dot(value, x_ref[...], TN).astype(BF)
        part = pl.ds(at, size)
        sent.append(pltpu.make_async_copy(grad_ref.at[part, :], grad_hbm.at[part, :], sems.at[slot + k]))
        sent[-1].start()
    return sent


def backward_hidden(mine, other, x, weight, near, far, lefts, sort, index):
    n, depth = weight.shape

    def body(m_ref, o_ref, x_ref, near_ref, far_ref, l_ref, s_ref, i_ref, w_ref, out_ref, grad_hbm, grad_ref, sems):
        sent = grads(m_ref, o_ref, 0, x_ref, grad_ref, grad_hbm, sems)
        total = through(m_ref, o_ref, 0, w_ref, near_ref, far_ref, l_ref, s_ref, 2)
        out_ref[...] = dot(pick(i_ref, SIZE), total.astype(BF), NN).astype(BF)
        for copy in sent:
            copy.wait()

    return pallas(
        body,
        "backward_hidden",
        (mine, other, x, near, far, lefts, sort, index, weight),
        [jax.ShapeDtypeStruct((SIZE, depth), BF), jax.ShapeDtypeStruct((n, depth), BF)],
        [VMEM] * 9,
        [VMEM, HBM],
        [pltpu.VMEM((n, depth), BF), pltpu.SemaphoreType.DMA((len(cuts(n, STEP)),))],
    )


def backward_pair(mine, other, gate_w, up_w, near, far, lefts, sort, index):
    n, depth = gate_w.shape
    wide = padded(n)

    def body(m_ref, o_ref, near_ref, far_ref, l_ref, s_ref, i_ref, gw_ref, uw_ref, out_ref):
        total = through(m_ref, o_ref, 0, gw_ref, near_ref, far_ref, l_ref, s_ref, 0)
        total = total + through(m_ref, o_ref, wide, uw_ref, near_ref, far_ref, l_ref, s_ref, 1)
        out_ref[...] = dot(pick(i_ref, SIZE), total.astype(BF), NN).astype(BF)

    return pallas(
        body,
        "backward_pair",
        (mine, other, near, far, lefts, sort, index, gate_w, up_w),
        jax.ShapeDtypeStruct((SIZE, depth), BF),
        [VMEM] * 9,
        VMEM,
        [],
    )


def weight_grad(mine, other, x, first, n):
    depth = x.shape[1]

    def body(m_ref, o_ref, x_ref, grad_hbm, grad_ref, sems):
        for copy in grads(m_ref, o_ref, first, x_ref, grad_ref, grad_hbm, sems):
            copy.wait()

    return pallas(
        body,
        "weight_grad",
        (mine, other, x),
        jax.ShapeDtypeStruct((n, depth), BF),
        [VMEM] * 3,
        HBM,
        [pltpu.VMEM((n, depth), BF), pltpu.SemaphoreType.DMA((len(cuts(n, STEP)),))],
    )


def row_send(x, dz, da, dc):
    pairs = []
    for z in range(4):
        for a in range(2):
            for c in range(2):
                to = ((z + dz) % 4) * 4 + ((a + da) % 2) * 2 + (c + dc) % 2
                pairs.append((z * 4 + a * 2 + c, to))
    return lax.ppermute(x, "row", pairs)


def col_send(x, dh, dy):
    pairs = []
    for h in range(2):
        for y in range(4):
            pairs.append((h * 4 + y, ((h + dh) % 2) * 4 + (y + dy) % 4))
    return lax.ppermute(x, "col", pairs)


def z_send(blocks):
    return [row_send(blocks[d].astype(BF), d, 0, 0) for d in (1, 3, 2)]


def z_spread(x):
    return [row_send(x, d, 0, 0) for d in (3, 2, 1)]


def x_send(x):
    return row_send(x, 0, 1, 0)


def core_send(x):
    return row_send(x, 0, 0, 1)


def pair_sum(mine, got):
    return (mine + got.astype(F32)).reshape(4, 2, ROWS, -1)


def plus(own, parts):
    for p in parts:
        own = own + p.astype(F32)
    return own


def shards(
    tokens,
    grad_out,
    gate_weight,
    up_weight,
    down_weight,
    gate_left,
    up_left,
    down_left,
    gate_right,
    up_right,
    down_right,
):
    n = gate_weight.shape[1]
    row, col = lax.axis_index("row"), lax.axis_index("col")
    z, a, c = row // 4, (row // 2) % 2, row % 2
    h, y = col // 4, col % 4
    z, a, c, h, y, tokens, grad_out, gate_weight, down_weight, *small = tie(
        *(z, a, c, h, y, tokens, grad_out, gate_weight, down_weight),
        *(gate_left, up_left, down_left, gate_right, up_right, down_right),
    )
    gate_left, up_left, down_left, gate_right, up_right, down_right = small

    k = jnp.arange(SIZE, dtype=jnp.int32)

    def owner(block):
        dc, dz, da = block // 8, (block // 2) % 4, block % 2
        return (z + dz) % 4 * 4 + (a + da) % 2 * 2 + (c + dc) % 2

    held = owner(k // ROWS) * ROWS + k % ROWS
    dest = (((h + k // 192) % 2) * 4 + (y + k // 48) % 4) * 48 + k % 48
    block = dest // ROWS
    dc, dz, da = (block % 2 - c) % 2, (block // 4 - z) % 4, ((block // 2) % 2 - a) % 2
    leave = ((dc * 4 + dz) * 2 + da) * ROWS + dest % ROWS
    held, leave = held[:, None], leave[:, None]
    j = jnp.arange(RANK, dtype=jnp.int32)
    sort = (j[:, None] == (owner(j // 8) * 8 + j % 8)[None, :]).astype(BF)
    my, mh, mt, mi = k // 96, (k // 48) % 2, (k // 16) % 3, k % 16
    rank = (((h - mh) % 2) * 4 + (y - my) % 4) * 16 + mi + RANK * mt
    match = (rank[None, :] == k[:, None]).astype(BF)

    gate_w, up_w, down_w = gate_weight.T, up_weight.T, down_weight.T
    edge = jnp.zeros((gate_right.shape[0], padded(n) - n), BF)
    rights = jnp.concatenate([gate_right, edge, up_right, edge, down_right, edge], axis=1)
    lefts = jnp.concatenate([gate_left.T, up_left.T, down_left.T], axis=0)
    lefts_h = col_send(lefts, 1, 0)
    held, sort, match, rights, lefts, lefts_h = tie(held, sort, match, rights, lefts, lefts_h)

    theirs, tok, out = forward_theirs(tokens, grad_out, held, gate_w, down_w)
    got = core_send(theirs)
    tok, rights = tie(tok, rights)
    rights_z = z_spread(rights)
    lefts = jnp.stack([lefts, lefts_h])
    lefts_y = [col_send(lefts, 0, d) for d in (1, 2, 3)]
    rights = jnp.stack([rights] + rights_z)
    rights_x = x_send(rights)

    pair, *sends = forward_mine(tok, out, gate_w, down_w, got)
    tok, pair = tie(tok, pair)
    pair_z = [row_send(sends[d - 1], d, 0, 0) for d in (1, 3, 2)]
    lefts = jnp.stack([lefts] + lefts_y).reshape(SIZE, -1)
    lefts = dot(match, lefts, NN).astype(BF)
    mine, theirs = forward_up(tok, out, lefts, up_w)
    got, rights_x = tie(core_send(theirs), rights_x)
    up = pair_sum(mine, got)
    up_x = x_send(up[:, 1].astype(BF))
    near = jnp.stack([rights, rights_x], axis=1).reshape(64, -1)
    far = core_send(near)

    *pair_z, up_x, leave = tie(*pair_z, up_x, leave)
    pair = plus(pair, pair_z).reshape(2, ROWS, -1)
    pair_x = x_send(pair[1].astype(BF))
    up = up[:, 0] + up_x.astype(F32)
    up_z = z_send(up)
    hidden, delta = act(pair[0], pair_x, up[0], up_z, near, far, sort, n)

    delta_x = x_send(delta)
    hidden_z = z_spread(hidden)
    delta_x, hidden_z = tie(delta_x, hidden_z)
    delta = jnp.stack([delta, delta_x])
    delta_z = z_spread(delta)
    hidden = jnp.stack([hidden] + hidden_z)
    hidden_x, delta_z = tie(x_send(hidden), delta_z)
    hidden = jnp.stack([hidden, hidden_x], axis=1).reshape(HALF, n)
    delta = jnp.stack([delta] + delta_z).reshape(HALF, -1)
    hidden_far, delta = tie(core_send(hidden), delta)
    delta_far = core_send(delta)
    mixed, down_grad = backward_hidden(hidden, hidden_far, out, down_w, near, far, lefts, sort, leave)
    mixed = mixed.reshape(2, 4, 48, -1)
    mixed_h = col_send(mixed[1], 1, 0)
    delta_far, mixed = tie(delta_far, mixed)
    input_grad = backward_pair(delta, delta_far, gate_w, up_w, near, far, lefts, sort, leave)
    input_grad = input_grad.reshape(2, 4, 48, -1)
    delta, leaving = tie(delta, input_grad[1])
    input_h = col_send(leaving, 1, 0)
    up_grad = weight_grad(delta, delta_far, tok, padded(n), n)
    input_h, delta, up_grad = tie(input_h, delta, up_grad)
    both = [mixed[0].astype(F32) + mixed_h.astype(F32), input_grad[0].astype(F32) + input_h.astype(F32)]
    leaving = [jnp.stack([part[d] for part in both]).astype(BF) for d in (1, 3, 2)]
    delta, *leaving = tie(delta, *leaving)
    both_y = [col_send(part, 0, d) for part, d in zip(leaving, (1, 3, 2))]
    gate_grad = weight_grad(delta, delta_far, tok, 0, n)
    both = [plus(both[t][0], [part[t] for part in both_y]).astype(BF) for t in range(2)]
    return both[0], both[1], gate_grad.T, up_grad.T, down_grad.T


def solution(mesh):
    arg = P("row", "col")
    in_specs = (P(None, "row"), P(None, "row")) + (arg,) * 9
    out_specs = (P("col", "row"), P("col", "row")) + (arg,) * 3
    return jax.shard_map(shards, mesh=mesh, in_specs=in_specs, out_specs=out_specs, check_vma=False)
```

```python
import jax
import jax.numpy as jnp
from jax import lax
from jax.experimental import pallas as pl
from jax.experimental.pallas import tpu as pltpu
from jax.sharding import PartitionSpec as P

BF = jnp.bfloat16
F32 = jnp.float32
ROWS = 24
HALF = 192
SIZE = 384
CHUNK = 1408
STEP = 512
RANK = 128

NN = ((1,), (0,))
NT = ((1,), (1,))
TN = ((0,), (0,))

VMEM = pl.BlockSpec(memory_space=pltpu.VMEM)
HBM = pl.BlockSpec(memory_space=pltpu.HBM)


def dot(a, b, dims):
    return lax.dot_general(a, b, (dims, ((), ())), preferred_element_type=F32)


def tie(*arrays):
    return lax.optimization_barrier(arrays)


def cuts(n, step):
    return [(at, min(step, n - at)) for at in range(0, n, step)]


def padded(n):
    return -(-n // 128) * 128


def pick(index_ref, size):
    return (index_ref[...] == lax.broadcasted_iota(jnp.int32, (size, size), 1)).astype(BF)


def pallas(body, name, ins, outs, in_specs, out_specs, scratch):
    return pl.pallas_call(
        body,
        out_shape=outs,
        in_specs=in_specs,
        out_specs=out_specs,
        scratch_shapes=scratch,
        compiler_params=pltpu.CompilerParams(vmem_limit_bytes=16 * 1024 * 1024),
        name=name,
    )(*ins)


def forward_theirs(tokens, grad_out, index, gate_w, down_w):
    n, depth = gate_w.shape
    wide = padded(n)

    def body(t_ref, g_ref, i_ref, gw_ref, dw_ref, theirs_ref, tok_ref, out_ref):
        theirs_ref[:, n:wide] = jnp.zeros((HALF, wide - n), BF)
        turn = pick(i_ref, SIZE)
        for in_ref, turned_ref, w_ref, first in ((t_ref, tok_ref, gw_ref, 0), (g_ref, out_ref, dw_ref, wide)):
            turned_ref[...] = dot(turn, in_ref[...], NN).astype(BF)
            for at, size in cuts(n, CHUNK):
                got = dot(turned_ref[HALF:, :], w_ref[at : at + size, :], NT)
                theirs_ref[:, first + at : first + at + size] = got.astype(BF)

    return pallas(
        body,
        "forward_theirs",
        (tokens, grad_out, index, gate_w, down_w),
        [jax.ShapeDtypeStruct((HALF, wide + n), BF)] + [jax.ShapeDtypeStruct((SIZE, depth), BF)] * 2,
        [VMEM] * 5,
        [VMEM] * 3,
        [],
    )


def forward_mine(tok, out, gate_w, down_w, got):
    n, depth = gate_w.shape
    wide = padded(n)
    quarter = HALF // 4

    def body(t_ref, o_ref, gw_ref, dw_ref, got_ref, own_ref, *send_refs):
        own_ref[:, n:wide] = jnp.zeros((quarter, wide - n), F32)
        for ref in send_refs:
            ref[:, n:wide] = jnp.zeros((quarter, wide - n), BF)
        for x_ref, w_ref, first in ((t_ref, gw_ref, 0), (o_ref, dw_ref, wide)):
            for at, size in cuts(n, CHUNK):
                part = slice(first + at, first + at + size)
                total = dot(x_ref[:HALF, :], w_ref[at : at + size, :], NT) + got_ref[:, part].astype(F32)
                own_ref[:, part] = total[:quarter]
                for d, ref in enumerate(send_refs, 1):
                    ref[:, part] = total[quarter * d : quarter * (d + 1)].astype(BF)

    return pallas(
        body,
        "forward_mine",
        (tok, out, gate_w, down_w, got),
        [jax.ShapeDtypeStruct((quarter, wide + n), F32)] + [jax.ShapeDtypeStruct((quarter, wide + n), BF)] * 3,
        [VMEM] * 5,
        [VMEM] * 4,
        [],
    )


def forward_up(tok, out, lefts, up_w):
    n, depth = up_w.shape
    low = 3 * RANK

    def body(t_ref, o_ref, l_ref, w_ref, mine_ref, theirs_ref):
        def put(at, size, got):
            mine_ref[:, at : at + size] = got[:HALF]
            theirs_ref[:, at : at + size] = got[HALF:].astype(BF)

        put(0, 2 * RANK, dot(t_ref[...], l_ref[: 2 * RANK, :], NT))
        put(2 * RANK, RANK, dot(o_ref[...], l_ref[2 * RANK :, :], NT))
        for at, size in cuts(n, CHUNK):
            put(low + at, size, dot(t_ref[...], w_ref[at : at + size, :], NT))

    return pallas(
        body,
        "forward_up",
        (tok, out, lefts, up_w),
        [jax.ShapeDtypeStruct((HALF, low + n), F32), jax.ShapeDtypeStruct((HALF, low + n), BF)],
        [VMEM] * 4,
        [VMEM] * 2,
        [],
    )


def act(pair, pair_x, up, parts, near, far, sort, n):
    wide = padded(n)
    low_n = 3 * RANK

    def body(p_ref, px_ref, u_ref, a_ref, b_ref, c_ref, near_ref, far_ref, sort_ref, hidden_ref, delta_ref):
        def total(at, size):
            part = slice(at, at + size)
            return u_ref[:, part] + a_ref[:, part].astype(F32) + b_ref[:, part].astype(F32) + c_ref[:, part].astype(F32)

        low = total(0, low_n).astype(BF)
        low = [dot(low[:, RANK * t : RANK * (t + 1)], sort_ref[...], NN).astype(BF) for t in range(3)]
        delta_ref[:, n:wide] = jnp.zeros((ROWS, wide - n), BF)
        for at, size in cuts(n, CHUNK):

            def more(t):
                part = slice(wide * t + at, wide * t + at + size)
                return dot(low[t], jnp.concatenate([near_ref[:, part], far_ref[:, part]], axis=0), NN)

            def both(first):
                part = slice(first + at, first + at + size)
                return p_ref[:, part] + px_ref[:, part].astype(F32)

            gate = both(0) + more(0)
            up_value = total(low_n + at, size) + more(1)
            back = both(wide) + more(2)
            sigma = jax.nn.sigmoid(gate)
            hidden_ref[:, at : at + size] = (gate * sigma * up_value).astype(BF)
            slope = sigma * (1.0 + gate * (1.0 - sigma))
            delta_ref[:, at : at + size] = (back * up_value * slope).astype(BF)
            delta_ref[:, wide + at : wide + at + size] = (back * gate * sigma).astype(BF)

    return pallas(
        body,
        "act",
        (pair, pair_x, up, *parts, near, far, sort),
        [jax.ShapeDtypeStruct((ROWS, n), BF), jax.ShapeDtypeStruct((ROWS, wide + n), BF)],
        [VMEM] * 9,
        [VMEM] * 2,
        [],
    )


def through(mine_ref, other_ref, first, w_ref, near_ref, far_ref, left_ref, sort_ref, place):
    n = w_ref.shape[0]
    wide = padded(n)
    total = low = None
    for at, size in cuts(n, CHUNK):
        part = slice(first + at, first + at + size)
        value = jnp.concatenate([mine_ref[:, part], other_ref[:, part]], axis=0)
        part = slice(wide * place + at, wide * place + at + size)
        right = jnp.concatenate([near_ref[:, part], far_ref[:, part]], axis=0)
        more = dot(value, right, NT)
        low = more if low is None else low + more
        more = dot(value, w_ref[at : at + size, :], NN)
        total = more if total is None else total + more
    low = dot(low.astype(BF), sort_ref[...], NT).astype(BF)
    return total + dot(low, left_ref[RANK * place : RANK * (place + 1), :], NN)


def grads(mine_ref, other_ref, first, x_ref, grad_ref, grad_hbm, sems, slot=0):
    n = grad_ref.shape[0]
    sent = []
    for k, (at, size) in enumerate(cuts(n, STEP)):
        part = slice(first + at, first + at + size)
        value = jnp.concatenate([mine_ref[:, part], other_ref[:, part]], axis=0)
        grad_ref[at : at + size, :] = dot(value, x_ref[...], TN).astype(BF)
        part = pl.ds(at, size)
        sent.append(pltpu.make_async_copy(grad_ref.at[part, :], grad_hbm.at[part, :], sems.at[slot + k]))
        sent[-1].start()
    return sent


def backward_hidden(mine, other, x, weight, near, far, lefts, sort, index):
    n, depth = weight.shape

    def body(m_ref, o_ref, x_ref, near_ref, far_ref, l_ref, s_ref, i_ref, w_ref, out_ref, grad_hbm, grad_ref, sems):
        sent = grads(m_ref, o_ref, 0, x_ref, grad_ref, grad_hbm, sems)
        total = through(m_ref, o_ref, 0, w_ref, near_ref, far_ref, l_ref, s_ref, 2)
        out_ref[...] = dot(pick(i_ref, SIZE), total.astype(BF), NN).astype(BF)
        for copy in sent:
            copy.wait()

    return pallas(
        body,
        "backward_hidden",
        (mine, other, x, near, far, lefts, sort, index, weight),
        [jax.ShapeDtypeStruct((SIZE, depth), BF), jax.ShapeDtypeStruct((n, depth), BF)],
        [VMEM] * 9,
        [VMEM, HBM],
        [pltpu.VMEM((n, depth), BF), pltpu.SemaphoreType.DMA((len(cuts(n, STEP)),))],
    )


def backward_pair(mine, other, gate_w, up_w, near, far, lefts, sort, index):
    n, depth = gate_w.shape
    wide = padded(n)

    def body(m_ref, o_ref, near_ref, far_ref, l_ref, s_ref, i_ref, gw_ref, uw_ref, out_ref):
        total = through(m_ref, o_ref, 0, gw_ref, near_ref, far_ref, l_ref, s_ref, 0)
        total = total + through(m_ref, o_ref, wide, uw_ref, near_ref, far_ref, l_ref, s_ref, 1)
        out_ref[...] = dot(pick(i_ref, SIZE), total.astype(BF), NN).astype(BF)

    return pallas(
        body,
        "backward_pair",
        (mine, other, near, far, lefts, sort, index, gate_w, up_w),
        jax.ShapeDtypeStruct((SIZE, depth), BF),
        [VMEM] * 9,
        VMEM,
        [],
    )


def weight_grad(mine, other, x, first, n):
    depth = x.shape[1]

    def body(m_ref, o_ref, x_ref, grad_hbm, grad_ref, sems):
        for copy in grads(m_ref, o_ref, first, x_ref, grad_ref, grad_hbm, sems):
            copy.wait()

    return pallas(
        body,
        "weight_grad",
        (mine, other, x),
        jax.ShapeDtypeStruct((n, depth), BF),
        [VMEM] * 3,
        HBM,
        [pltpu.VMEM((n, depth), BF), pltpu.SemaphoreType.DMA((len(cuts(n, STEP)),))],
    )


def row_send(x, dz, da, dc):
    pairs = []
    for z in range(4):
        for a in range(2):
            for c in range(2):
                to = ((z + dz) % 4) * 4 + ((a + da) % 2) * 2 + (c + dc) % 2
                pairs.append((z * 4 + a * 2 + c, to))
    return lax.ppermute(x, "row", pairs)


def col_send(x, dh, dy):
    pairs = []
    for h in range(2):
        for y in range(4):
            pairs.append((h * 4 + y, ((h + dh) % 2) * 4 + (y + dy) % 4))
    return lax.ppermute(x, "col", pairs)


def z_send(blocks):
    return [row_send(blocks[d].astype(BF), d, 0, 0) for d in (1, 3, 2)]


def swap(x, axis, bit):
    step = 4 * bit if axis == "row" else bit
    return lax.ppermute(x, axis, [(i, i ^ step) for i in range(16 if axis == "row" else 8)])


def z_spread(x):
    return [row_send(x, d, 0, 0) for d in (3, 2, 1)]


def x_send(x):
    return row_send(x, 0, 1, 0)


def core_send(x):
    return row_send(x, 0, 0, 1)


def pair_sum(mine, got):
    return (mine + got.astype(F32)).reshape(4, 2, ROWS, -1)


def plus(own, parts):
    for p in parts:
        own = own + p.astype(F32)
    return own


def shards(
    tokens,
    grad_out,
    gate_weight,
    up_weight,
    down_weight,
    gate_left,
    up_left,
    down_left,
    gate_right,
    up_right,
    down_right,
):
    n = gate_weight.shape[1]
    row, col = lax.axis_index("row"), lax.axis_index("col")
    z, a, c = row // 4, (row // 2) % 2, row % 2
    h, y = col // 4, col % 4
    z, a, c, h, y, tokens, grad_out, gate_weight, down_weight, *small = tie(
        *(z, a, c, h, y, tokens, grad_out, gate_weight, down_weight),
        *(gate_left, up_left, down_left, gate_right, up_right, down_right),
    )
    gate_left, up_left, down_left, gate_right, up_right, down_right = small

    k = jnp.arange(SIZE, dtype=jnp.int32)

    def owner(block):
        dc, dz, da = block // 8, (block // 2) % 4, block % 2
        return (z + dz) % 4 * 4 + (a + da) % 2 * 2 + (c + dc) % 2

    held = owner(k // ROWS) * ROWS + k % ROWS
    dest = (((h + k // 192) % 2) * 4 + (y + k // 48) % 4) * 48 + k % 48
    block = dest // ROWS
    dc, dz, da = (block % 2 - c) % 2, (block // 4 - z) % 4, ((block // 2) % 2 - a) % 2
    leave = ((dc * 4 + dz) * 2 + da) * ROWS + dest % ROWS
    held, leave = held[:, None], leave[:, None]
    j = jnp.arange(RANK, dtype=jnp.int32)
    block = j // 8
    dc, ez, da = block // 8, (block // 2) % 4, block % 2
    source = (z ^ ez) * 4 + (a + da) % 2 * 2 + (c + dc) % 2
    sort = (j[:, None] == (source * 8 + j % 8)[None, :]).astype(BF)
    my, mh, mt, mi = k // 96, (k // 48) % 2, (k // 16) % 3, k % 16
    rank = (((h - mh) % 2) * 4 + (y ^ my)) * 16 + mi + RANK * mt
    match = (rank[None, :] == k[:, None]).astype(BF)

    gate_w, up_w, down_w = gate_weight.T, up_weight.T, down_weight.T
    edge = jnp.zeros((gate_right.shape[0], padded(n) - n), BF)
    rights = jnp.concatenate([gate_right, edge, up_right, edge, down_right, edge], axis=1)
    lefts = jnp.concatenate([gate_left.T, up_left.T, down_left.T], axis=0)
    lefts_h = col_send(lefts, 1, 0)
    held, sort, match, rights, lefts, lefts_h = tie(held, sort, match, rights, lefts, lefts_h)

    theirs, tok, out = forward_theirs(tokens, grad_out, held, gate_w, down_w)
    got = core_send(theirs)
    tok, rights = tie(tok, rights)
    lefts = jnp.stack([lefts, lefts_h])
    lefts = jnp.stack([lefts, swap(lefts, "col", 1)])
    rights = jnp.stack([rights, swap(rights, "row", 1)])
    lefts = jnp.stack([lefts, swap(lefts, "col", 2)])
    rights = jnp.stack([rights, swap(rights, "row", 2)]).reshape(4, *rights.shape[1:])
    rights_x = x_send(rights)

    pair, *sends = forward_mine(tok, out, gate_w, down_w, got)
    tok, pair = tie(tok, pair)
    pair_z = [row_send(sends[d - 1], d, 0, 0) for d in (1, 3, 2)]
    lefts = lefts.reshape(SIZE, -1)
    lefts = dot(match, lefts, NN).astype(BF)
    mine, theirs = forward_up(tok, out, lefts, up_w)
    got, rights_x = tie(core_send(theirs), rights_x)
    up = pair_sum(mine, got)
    up_x = x_send(up[:, 1].astype(BF))
    near = jnp.stack([rights, rights_x], axis=1).reshape(64, -1)
    far = core_send(near)

    *pair_z, up_x, leave = tie(*pair_z, up_x, leave)
    pair = plus(pair, pair_z).reshape(2, ROWS, -1)
    pair_x = x_send(pair[1].astype(BF))
    up = up[:, 0] + up_x.astype(F32)
    up_z = z_send(up)
    hidden, delta = act(pair[0], pair_x, up[0], up_z, near, far, sort, n)

    delta_x = x_send(delta)
    hidden_z = z_spread(hidden)
    delta_x, hidden_z = tie(delta_x, hidden_z)
    delta = jnp.stack([delta, delta_x])
    delta_z = z_spread(delta)
    hidden = jnp.stack([hidden] + hidden_z)
    hidden_x, delta_z = tie(x_send(hidden), delta_z)
    hidden = jnp.stack([hidden, hidden_x], axis=1).reshape(HALF, n)
    delta = jnp.stack([delta] + delta_z).reshape(HALF, -1)
    hidden_far, delta = tie(core_send(hidden), delta)
    delta_far = core_send(delta)
    mixed, down_grad = backward_hidden(hidden, hidden_far, out, down_w, near, far, lefts, sort, leave)
    mixed = mixed.reshape(2, 4, 48, -1)
    mixed_h = col_send(mixed[1], 1, 0)
    delta_far, mixed = tie(delta_far, mixed)
    input_grad = backward_pair(delta, delta_far, gate_w, up_w, near, far, lefts, sort, leave)
    input_grad = input_grad.reshape(2, 4, 48, -1)
    delta, leaving = tie(delta, input_grad[1])
    input_h = col_send(leaving, 1, 0)
    up_grad = weight_grad(delta, delta_far, tok, padded(n), n)
    input_h, delta, up_grad = tie(input_h, delta, up_grad)
    both = [mixed[0].astype(F32) + mixed_h.astype(F32), input_grad[0].astype(F32) + input_h.astype(F32)]
    leaving = [jnp.stack([part[d] for part in both]).astype(BF) for d in (1, 3, 2)]
    delta, *leaving = tie(delta, *leaving)
    both_y = [col_send(part, 0, d) for part, d in zip(leaving, (1, 3, 2))]
    gate_grad = weight_grad(delta, delta_far, tok, 0, n)
    both = [plus(both[t][0], [part[t] for part in both_y]).astype(BF) for t in range(2)]
    return both[0], both[1], gate_grad.T, up_grad.T, down_grad.T


def solution(mesh):
    arg = P("row", "col")
    in_specs = (P(None, "row"), P(None, "row")) + (arg,) * 9
    out_specs = (P("col", "row"), P("col", "row")) + (arg,) * 3
    return jax.shard_map(shards, mesh=mesh, in_specs=in_specs, out_specs=out_specs, check_vma=False)
```

```python
import jax
import jax.numpy as jnp
from jax import lax
from jax.experimental import pallas as pl
from jax.experimental.pallas import tpu as pltpu
from jax.sharding import PartitionSpec as P

BF = jnp.bfloat16
F32 = jnp.float32
ROWS = 24
HALF = 192
SIZE = 384
CHUNK = 1408
STEP = 512
RANK = 128

NN = ((1,), (0,))
NT = ((1,), (1,))
TN = ((0,), (0,))

VMEM = pl.BlockSpec(memory_space=pltpu.VMEM)
HBM = pl.BlockSpec(memory_space=pltpu.HBM)


def dot(a, b, dims):
    return lax.dot_general(a, b, (dims, ((), ())), preferred_element_type=F32)


def tie(*arrays):
    return lax.optimization_barrier(arrays)


def cuts(n, step):
    return [(at, min(step, n - at)) for at in range(0, n, step)]


def padded(n):
    return -(-n // 128) * 128


def pick(index_ref, size):
    return (index_ref[...] == lax.broadcasted_iota(jnp.int32, (size, size), 1)).astype(BF)


def pallas(body, name, ins, outs, in_specs, out_specs, scratch):
    return pl.pallas_call(
        body,
        out_shape=outs,
        in_specs=in_specs,
        out_specs=out_specs,
        scratch_shapes=scratch,
        compiler_params=pltpu.CompilerParams(vmem_limit_bytes=16 * 1024 * 1024),
        name=name,
    )(*ins)


def forward_theirs(tokens, grad_out, index, gate_w, down_w):
    n, depth = gate_w.shape
    wide = padded(n)

    def body(t_ref, g_ref, i_ref, gw_ref, dw_ref, theirs_ref, tok_ref, out_ref):
        theirs_ref[:, n:wide] = jnp.zeros((HALF, wide - n), BF)
        turn = pick(i_ref, SIZE)
        for in_ref, turned_ref, w_ref, first in ((t_ref, tok_ref, gw_ref, 0), (g_ref, out_ref, dw_ref, wide)):
            turned_ref[...] = dot(turn, in_ref[...], NN).astype(BF)
            for at, size in cuts(n, CHUNK):
                got = dot(turned_ref[HALF:, :], w_ref[at : at + size, :], NT)
                theirs_ref[:, first + at : first + at + size] = got.astype(BF)

    return pallas(
        body,
        "forward_theirs",
        (tokens, grad_out, index, gate_w, down_w),
        [jax.ShapeDtypeStruct((HALF, wide + n), BF)] + [jax.ShapeDtypeStruct((SIZE, depth), BF)] * 2,
        [VMEM] * 5,
        [VMEM] * 3,
        [],
    )


def forward_mine(tok, out, gate_w, down_w, got):
    n, depth = gate_w.shape
    wide = padded(n)
    quarter = HALF // 4

    def body(t_ref, o_ref, gw_ref, dw_ref, got_ref, own_ref, *send_refs):
        own_ref[:, n:wide] = jnp.zeros((quarter, wide - n), F32)
        for ref in send_refs:
            ref[:, n:wide] = jnp.zeros((quarter, wide - n), BF)
        for x_ref, w_ref, first in ((t_ref, gw_ref, 0), (o_ref, dw_ref, wide)):
            for at, size in cuts(n, CHUNK):
                part = slice(first + at, first + at + size)
                total = dot(x_ref[:HALF, :], w_ref[at : at + size, :], NT) + got_ref[:, part].astype(F32)
                own_ref[:, part] = total[:quarter]
                for d, ref in enumerate(send_refs, 1):
                    ref[:, part] = total[quarter * d : quarter * (d + 1)].astype(BF)

    return pallas(
        body,
        "forward_mine",
        (tok, out, gate_w, down_w, got),
        [jax.ShapeDtypeStruct((quarter, wide + n), F32)] + [jax.ShapeDtypeStruct((quarter, wide + n), BF)] * 3,
        [VMEM] * 5,
        [VMEM] * 4,
        [],
    )


def forward_up(tok, out, lefts, up_w):
    n, depth = up_w.shape
    low = 3 * RANK

    def body(t_ref, o_ref, l_ref, w_ref, mine_ref, theirs_ref):
        def put(at, size, got):
            mine_ref[:, at : at + size] = got[:HALF]
            theirs_ref[:, at : at + size] = got[HALF:].astype(BF)

        put(0, 2 * RANK, dot(t_ref[...], l_ref[: 2 * RANK, :], NT))
        put(2 * RANK, RANK, dot(o_ref[...], l_ref[2 * RANK :, :], NT))
        for at, size in cuts(n, CHUNK):
            put(low + at, size, dot(t_ref[...], w_ref[at : at + size, :], NT))

    return pallas(
        body,
        "forward_up",
        (tok, out, lefts, up_w),
        [jax.ShapeDtypeStruct((HALF, low + n), F32), jax.ShapeDtypeStruct((HALF, low + n), BF)],
        [VMEM] * 4,
        [VMEM] * 2,
        [],
    )


def act(pair, pair_x, up, parts, near, far, sort, n):
    wide = padded(n)
    low_n = 3 * RANK

    def body(p_ref, px_ref, u_ref, a_ref, b_ref, c_ref, near_ref, far_ref, sort_ref, hidden_ref, delta_ref):
        def total(at, size):
            part = slice(at, at + size)
            return u_ref[:, part] + a_ref[:, part].astype(F32) + b_ref[:, part].astype(F32) + c_ref[:, part].astype(F32)

        low = total(0, low_n).astype(BF)
        low = [dot(low[:, RANK * t : RANK * (t + 1)], sort_ref[...], NN).astype(BF) for t in range(3)]
        delta_ref[:, n:wide] = jnp.zeros((ROWS, wide - n), BF)
        for at, size in cuts(n, CHUNK):

            def more(t):
                part = slice(wide * t + at, wide * t + at + size)
                return dot(low[t], jnp.concatenate([near_ref[:, part], far_ref[:, part]], axis=0), NN)

            def both(first):
                part = slice(first + at, first + at + size)
                return p_ref[:, part] + px_ref[:, part].astype(F32)

            gate = both(0) + more(0)
            up_value = total(low_n + at, size) + more(1)
            back = both(wide) + more(2)
            sigma = jax.nn.sigmoid(gate)
            hidden_ref[:, at : at + size] = (gate * sigma * up_value).astype(BF)
            slope = sigma * (1.0 + gate * (1.0 - sigma))
            delta_ref[:, at : at + size] = (back * up_value * slope).astype(BF)
            delta_ref[:, wide + at : wide + at + size] = (back * gate * sigma).astype(BF)

    return pallas(
        body,
        "act",
        (pair, pair_x, up, *parts, near, far, sort),
        [jax.ShapeDtypeStruct((ROWS, n), BF), jax.ShapeDtypeStruct((ROWS, wide + n), BF)],
        [VMEM] * 9,
        [VMEM] * 2,
        [],
    )


def through(mine_ref, other_ref, first, w_ref, near_ref, far_ref, left_ref, sort_ref, place):
    n = w_ref.shape[0]
    wide = padded(n)
    total = low = None
    for at, size in cuts(n, CHUNK):
        part = slice(first + at, first + at + size)
        value = jnp.concatenate([mine_ref[:, part], other_ref[:, part]], axis=0)
        part = slice(wide * place + at, wide * place + at + size)
        right = jnp.concatenate([near_ref[:, part], far_ref[:, part]], axis=0)
        more = dot(value, right, NT)
        low = more if low is None else low + more
        more = dot(value, w_ref[at : at + size, :], NN)
        total = more if total is None else total + more
    low = dot(low.astype(BF), sort_ref[...], NT).astype(BF)
    return total + dot(low, left_ref[RANK * place : RANK * (place + 1), :], NN)


def grads(mine_ref, other_ref, first, x_ref, grad_ref, grad_hbm, sems, slot=0):
    n = grad_ref.shape[0]
    sent = []
    for k, (at, size) in enumerate(cuts(n, STEP)):
        part = slice(first + at, first + at + size)
        value = jnp.concatenate([mine_ref[:, part], other_ref[:, part]], axis=0)
        grad_ref[at : at + size, :] = dot(value, x_ref[...], TN).astype(BF)
        part = pl.ds(at, size)
        sent.append(pltpu.make_async_copy(grad_ref.at[part, :], grad_hbm.at[part, :], sems.at[slot + k]))
        sent[-1].start()
    return sent


def backward_hidden(mine, other, weight, near, far, lefts, sort, index):
    def body(m_ref, o_ref, near_ref, far_ref, l_ref, s_ref, i_ref, w_ref, out_ref):
        total = through(m_ref, o_ref, 0, w_ref, near_ref, far_ref, l_ref, s_ref, 2)
        out_ref[...] = dot(pick(i_ref, SIZE), total.astype(BF), NN).astype(BF)

    return pallas(
        body,
        "backward_hidden",
        (mine, other, near, far, lefts, sort, index, weight),
        jax.ShapeDtypeStruct((SIZE, weight.shape[1]), BF),
        [VMEM] * 8,
        VMEM,
        [],
    )


def backward_pair(mine, other, gate_w, up_w, near, far, lefts, sort, index):
    n, depth = gate_w.shape
    wide = padded(n)

    def body(m_ref, o_ref, near_ref, far_ref, l_ref, s_ref, i_ref, gw_ref, uw_ref, out_ref):
        total = through(m_ref, o_ref, 0, gw_ref, near_ref, far_ref, l_ref, s_ref, 0)
        total = total + through(m_ref, o_ref, wide, uw_ref, near_ref, far_ref, l_ref, s_ref, 1)
        out_ref[...] = dot(pick(i_ref, SIZE), total.astype(BF), NN).astype(BF)

    return pallas(
        body,
        "backward_pair",
        (mine, other, near, far, lefts, sort, index, gate_w, up_w),
        jax.ShapeDtypeStruct((SIZE, depth), BF),
        [VMEM] * 9,
        VMEM,
        [],
    )


def weight_grad(mine, other, x, first, n):
    depth = x.shape[1]

    def body(m_ref, o_ref, x_ref, grad_hbm, grad_ref, sems):
        for copy in grads(m_ref, o_ref, first, x_ref, grad_ref, grad_hbm, sems):
            copy.wait()

    return pallas(
        body,
        "weight_grad",
        (mine, other, x),
        jax.ShapeDtypeStruct((n, depth), BF),
        [VMEM] * 3,
        HBM,
        [pltpu.VMEM((n, depth), BF), pltpu.SemaphoreType.DMA((len(cuts(n, STEP)),))],
    )


def row_send(x, dz, da, dc):
    pairs = []
    for z in range(4):
        for a in range(2):
            for c in range(2):
                to = ((z + dz) % 4) * 4 + ((a + da) % 2) * 2 + (c + dc) % 2
                pairs.append((z * 4 + a * 2 + c, to))
    return lax.ppermute(x, "row", pairs)


def col_send(x, dh, dy):
    pairs = []
    for h in range(2):
        for y in range(4):
            pairs.append((h * 4 + y, ((h + dh) % 2) * 4 + (y + dy) % 4))
    return lax.ppermute(x, "col", pairs)


def z_send(blocks):
    return [row_send(blocks[d].astype(BF), d, 0, 0) for d in (1, 3, 2)]


def z_spread(x):
    return [row_send(x, d, 0, 0) for d in (3, 2, 1)]


def x_send(x):
    return row_send(x, 0, 1, 0)


def core_send(x):
    return row_send(x, 0, 0, 1)


def pair_sum(mine, got):
    return (mine + got.astype(F32)).reshape(4, 2, ROWS, -1)


def plus(own, parts):
    for p in parts:
        own = own + p.astype(F32)
    return own


def shards(
    tokens,
    grad_out,
    gate_weight,
    up_weight,
    down_weight,
    gate_left,
    up_left,
    down_left,
    gate_right,
    up_right,
    down_right,
):
    n = gate_weight.shape[1]
    row, col = lax.axis_index("row"), lax.axis_index("col")
    z, a, c = row // 4, (row // 2) % 2, row % 2
    h, y = col // 4, col % 4
    z, a, c, h, y, tokens, grad_out, gate_weight, down_weight, *small = tie(
        *(z, a, c, h, y, tokens, grad_out, gate_weight, down_weight),
        *(gate_left, up_left, down_left, gate_right, up_right, down_right),
    )
    gate_left, up_left, down_left, gate_right, up_right, down_right = small

    k = jnp.arange(SIZE, dtype=jnp.int32)

    def owner(block):
        dc, dz, da = block // 8, (block // 2) % 4, block % 2
        return (z + dz) % 4 * 4 + (a + da) % 2 * 2 + (c + dc) % 2

    held = owner(k // ROWS) * ROWS + k % ROWS
    dest = (((h + k // 192) % 2) * 4 + (y + k // 48) % 4) * 48 + k % 48
    block = dest // ROWS
    dc, dz, da = (block % 2 - c) % 2, (block // 4 - z) % 4, ((block // 2) % 2 - a) % 2
    leave = ((dc * 4 + dz) * 2 + da) * ROWS + dest % ROWS
    held, leave = held[:, None], leave[:, None]
    j = jnp.arange(RANK, dtype=jnp.int32)
    sort = (j[:, None] == (owner(j // 8) * 8 + j % 8)[None, :]).astype(BF)
    my, mh, mt, mi = k // 96, (k // 48) % 2, (k // 16) % 3, k % 16
    rank = (((h - mh) % 2) * 4 + (y - my) % 4) * 16 + mi + RANK * mt
    match = (rank[None, :] == k[:, None]).astype(BF)

    gate_w, up_w, down_w = gate_weight.T, up_weight.T, down_weight.T
    edge = jnp.zeros((gate_right.shape[0], padded(n) - n), BF)
    rights = jnp.concatenate([gate_right, edge, up_right, edge, down_right, edge], axis=1)
    lefts = jnp.concatenate([gate_left.T, up_left.T, down_left.T], axis=0)
    lefts_h = col_send(lefts, 1, 0)
    held, sort, match, rights, lefts, lefts_h = tie(held, sort, match, rights, lefts, lefts_h)

    theirs, tok, out = forward_theirs(tokens, grad_out, held, gate_w, down_w)
    got = core_send(theirs)
    tok, rights = tie(tok, rights)
    rights_z = z_spread(rights)
    lefts = jnp.stack([lefts, lefts_h])
    lefts_y = [col_send(lefts, 0, d) for d in (1, 2, 3)]
    rights = jnp.stack([rights] + rights_z)
    rights_x = x_send(rights)

    pair, *sends = forward_mine(tok, out, gate_w, down_w, got)
    tok, pair = tie(tok, pair)
    pair_z = [row_send(sends[d - 1], d, 0, 0) for d in (1, 3, 2)]
    lefts = jnp.stack([lefts] + lefts_y).reshape(SIZE, -1)
    lefts = dot(match, lefts, NN).astype(BF)
    mine, theirs = forward_up(tok, out, lefts, up_w)
    got, rights_x = tie(core_send(theirs), rights_x)
    up = pair_sum(mine, got)
    up_x = x_send(up[:, 1].astype(BF))
    near = jnp.stack([rights, rights_x], axis=1).reshape(64, -1)
    far = core_send(near)

    *pair_z, up_x = tie(*pair_z, up_x)
    pair = plus(pair, pair_z).reshape(2, ROWS, -1)
    pair_x = x_send(pair[1].astype(BF))
    up = up[:, 0] + up_x.astype(F32)
    up_z = z_send(up)
    hidden, delta = act(pair[0], pair_x, up[0], up_z, near, far, sort, n)

    delta_x = x_send(delta)
    hidden_z = z_spread(hidden)
    delta_x, hidden_z = tie(delta_x, hidden_z)
    delta = jnp.stack([delta, delta_x])
    delta_z = z_spread(delta)
    hidden = jnp.stack([hidden] + hidden_z)
    hidden_x, delta_z = tie(x_send(hidden), delta_z)
    hidden = jnp.stack([hidden, hidden_x], axis=1).reshape(HALF, n)
    delta = jnp.stack([delta] + delta_z).reshape(HALF, -1)
    hidden_far, delta = tie(core_send(hidden), delta)
    delta_far = core_send(delta)
    mixed = backward_hidden(hidden, hidden_far, down_w, near, far, lefts, sort, leave)
    mixed = mixed.reshape(2, 4, 48, -1)
    mixed_h = col_send(mixed[1], 1, 0)
    delta_far, mixed = tie(delta_far, mixed)
    input_grad = backward_pair(delta, delta_far, gate_w, up_w, near, far, lefts, sort, leave)
    input_grad = input_grad.reshape(2, 4, 48, -1)
    delta, hidden, leaving = tie(delta, hidden, input_grad[1])
    input_h = col_send(leaving, 1, 0)
    up_grad = weight_grad(delta, delta_far, tok, padded(n), n)
    down_grad = weight_grad(hidden, hidden_far, out, 0, n)
    input_h, delta, up_grad, down_grad = tie(input_h, delta, up_grad, down_grad)
    both = [mixed[0].astype(F32) + mixed_h.astype(F32), input_grad[0].astype(F32) + input_h.astype(F32)]
    leaving = [jnp.stack([part[d] for part in both]).astype(BF) for d in (1, 3, 2)]
    delta, *leaving = tie(delta, *leaving)
    both_y = [col_send(part, 0, d) for part, d in zip(leaving, (1, 3, 2))]
    gate_grad = weight_grad(delta, delta_far, tok, 0, n)
    both = [plus(both[t][0], [part[t] for part in both_y]).astype(BF) for t in range(2)]
    return both[0], both[1], gate_grad.T, up_grad.T, down_grad.T


def solution(mesh):
    arg = P("row", "col")
    in_specs = (P(None, "row"), P(None, "row")) + (arg,) * 9
    out_specs = (P("col", "row"), P("col", "row")) + (arg,) * 3
    return jax.shard_map(shards, mesh=mesh, in_specs=in_specs, out_specs=out_specs, check_vma=False)
```
